32 devices in a mesh: outer: 4 (over y, x), inner: 8 (over z, core).
Axes of the slice: x: 2, y: 2, z: 4, core: 2. Of those that a mesh axis runs over, the one named last changes fastest.
Arguments:
- queries: bfloat16 [8192, 1024], P(('outer', 'inner')), may hold values from -480 to 480
- keys: bfloat16 [8192, 512], P(('outer', 'inner')), may hold values from -8 to 8
- values: bfloat16 [8192, 512], P(('outer', 'inner')), may hold values from -4 to 4
- residual: bfloat16 [8192, 1024], P(('outer', 'inner')), may hold values from -5 to 5
- norm_gain: float32 [1024], replicated, may hold values from 0.1 to 1.9
- w_gate: bfloat16 [8, 1024, 512], P('inner'), may hold values from -0.1875 to 0.1875
- w_up: bfloat16 [8, 1024, 512], P('inner'), may hold values from -0.1875 to 0.1875
- w_down: bfloat16 [8, 512, 1024], P('inner'), may hold values from -0.25 to 0.25
- routes: int32 [8192, 2], P(('outer', 'inner')), may hold values from 0 to 7, all different within a row; in each aligned block of 256 rows (0 to 255, 256 to 511, ...) at most 128 rows name the same one
- gates: float32 [8192, 2], P(('outer', 'inner')), may hold values from 0.2 to 1
Outputs:
- layer_out: bfloat16 [8192, 1024], P(('outer', 'inner'))
The draws below stay inside these ranges and needn't reach their ends.
Inputs may be any that keep to these rules, and one draw needn't show every extreme that they name: `routes`: A patch's two experts differ. Within one block of 256 patches no expert is picked more than 128 times, and in some block one expert is picked exactly 128 times.
All inputs are finite; a program needn't handle non-finite values.
Results may differ from the reference program's by a relative error of at most 0.0085.
Values may be sent and summed in bfloat16 or wider, within the bound.
A program may use at most 64 MiB of HBM per device.

```python
import math
import jax
import jax.numpy as jnp
import numpy as np
from jax import lax

D = 1024
QH = 8
KVH = 4
DH = 128
FF = 512
BACK = 3
TOK_DEV = 256
EXPERTS = 8
CAP = 128
TOKENS = 8192


def paired_draw(key):
    folded = jax.random.fold_in(key, 4471)
    key_q, key_k = jax.random.split(folded)
    query_draw = 1.7 * jax.random.truncated_normal(key_q, -4.5, 4.5, (TOKENS, QH * DH), jnp.float32)
    key_draw = 1.7 * jax.random.truncated_normal(key_k, -4.5, 4.5, (TOKENS, KVH * DH), jnp.float32)
    return (query_draw, key_draw)


def draw_queries(key, part):
    return paired_draw(key)[0].astype(jnp.bfloat16)


def draw_keys(key, part):
    return paired_draw(key)[1].astype(jnp.bfloat16)


def levels(stream_key, shape, shards, least, high):
    def one(axis_at, shards_of):
        heights = jax.random.uniform(jax.random.fold_in(jax.random.fold_in(stream_key, 6), axis_at), (shards_of,), jnp.float32, least / len(shards), high / len(shards))
        return jnp.repeat(jnp.exp(heights), shape[axis_at] // shards_of).reshape((-1,) + (1,) * (len(shape) - axis_at - 1))

    gain = one(*shards[0])
    for cut in shards[1:]:
        gain = gain * one(*cut)
    return gain


def assign_block(key, own, number, rows, count, top, reach, slope):
    sequence = jax.random.permutation(key, count)
    heavy_load, usual = load_shares(count, rows * top, reach, slope, True), load_shares(count, rows * top, reach, slope, False)
    places = jnp.arange(count)

    def named(tallies, turn):
        used = int((tallies > 0).sum())
        fixed = max(1, used // 4)
        shifted = fixed + (places - fixed + turn * (used - fixed)) % max(1, count - fixed)
        return jnp.zeros((count,), jnp.int32).at[sequence[jnp.where(places < fixed, places, shifted)]].set(jnp.asarray(tallies, jnp.int32))

    tallies = jnp.where(number % 4 == 0, named(heavy_load, number // 4), named(usual, number - number // 4 - 1))
    mixed = jax.random.permutation(jax.random.fold_in(own, 3), count)
    donor, taker = mixed[0:count // 2 * 2:2], mixed[1:count // 2 * 2:2]
    room = jnp.minimum(tallies[donor] - 1, reach - tallies[taker]) // 2
    room = jnp.where((donor == sequence[0]) | (taker == sequence[0]) | (tallies[taker] == 0), 0, jnp.maximum(room, 0))
    shifted = jax.random.randint(jax.random.fold_in(own, 4), (count // 2,), 0, 1 << 20) % (room + 1)
    tallies = tallies.at[donor].add(-shifted).at[taker].add(shifted)
    labels = jnp.searchsorted(jnp.cumsum(tallies), jnp.arange(rows * top), side="right").astype(jnp.int32)
    table = labels.reshape(top, rows).T
    table = table[jax.random.permutation(jax.random.fold_in(own, 1), rows)]
    turn = jax.random.randint(jax.random.fold_in(own, 2), (rows, 1), 0, top)
    return jnp.take_along_axis(table, (jnp.arange(top)[None, :] + turn) % top, axis=1)


def load_shares(amount, total, limit, lean, full):
    portions = [(1 << 20) // math.isqrt(rank ** lean) + 1 for rank in range(1, amount + 1)]
    largest = limit if full else min(limit, max(-(-total // amount), total * portions[0] // sum(portions)))
    least = 1 if total - largest >= amount - 1 else 0
    counts, surplus = [largest] + [least] * (amount - 1), total - largest - least * (amount - 1)
    while surplus > 0:
        candidates = [i for i in range(1, amount) if counts[i] < largest] or [i for i in range(1, amount) if counts[i] < limit]
        pool, left = sum([portions[i] for i in candidates]), surplus
        for i in candidates:
            extra = min(limit - counts[i], max(1, left * portions[i] // pool), surplus)
            counts[i] = counts[i] + extra
            surplus = surplus - extra
    return np.array(counts)


def gaussian(own_key, dims, width, limit, pieces=(), kind=jnp.bfloat16):
    factor_of = levels(own_key, dims, pieces, -0.22, 0.18) if pieces else 1.0
    entries = jax.random.normal(own_key, dims, jnp.float32) * width * factor_of
    return jnp.minimum(jnp.maximum(entries, -limit), limit).astype(kind)


def setup_inputs(seed: int = 0) -> dict:
    splits = jax.random.split(jax.random.key(seed), 11)
    queries = draw_queries(jax.random.fold_in(splits[10], 71), 0)
    keys = draw_keys(jax.random.fold_in(splits[10], 71), 0)
    values = gaussian(splits[2], (TOKENS, KVH * DH), 1.0, 4.0, ((0, 32),))
    residual = gaussian(splits[3], (TOKENS, D), 1.0, 5.0, ((0, 32),))
    norm_gain = jnp.clip(1.0 + 0.18 * jax.random.normal(splits[4], (D,), jnp.float32), 0.1, 1.9)
    w_gate = gaussian(splits[5], (EXPERTS, D, FF), D ** -0.5, 0.1875, ((0, 8),))
    w_up = gaussian(splits[6], (EXPERTS, D, FF), D ** -0.5, 0.1875, ((0, 8),))
    w_down = gaussian(splits[7], (EXPERTS, FF, D), FF ** -0.5, 0.25, ((0, 8),))
    routes_keys = jax.random.split(jax.random.fold_in(splits[8], 1), TOKENS // TOK_DEV)
    routes_turns = jax.random.permutation(jax.random.fold_in(splits[8], 3), TOKENS // TOK_DEV)
    routes = jax.vmap(lambda own, number: assign_block(jax.random.fold_in(splits[8], 2), own, number, TOK_DEV, EXPERTS, 2, CAP, 2))(routes_keys, routes_turns).reshape((TOKENS, 2))
    gates = jnp.clip(0.2 + 0.8 * jax.random.uniform(splits[9], (TOKENS, 2), jnp.float32) ** levels(splits[9], (TOKENS, 2), ((0, 32),), -0.2, 0.2), 0.2, 1.0)
    return dict(queries=queries, keys=keys, values=values, residual=residual, norm_gain=norm_gain, w_gate=w_gate, w_up=w_up, w_down=w_down, routes=routes, gates=gates)


def feed_forward(rows, gate_matrix, up_matrix, down_matrix):
    gate_part = jnp.dot(rows, gate_matrix, preferred_element_type=jnp.float32)
    up_part = jnp.dot(rows, up_matrix, preferred_element_type=jnp.float32)
    inner_act = (jax.nn.silu(gate_part) * up_part).astype(jnp.bfloat16)
    return jnp.dot(inner_act, down_matrix, preferred_element_type=jnp.float32).astype(jnp.bfloat16)

def reference(queries, keys, values, residual, norm_gain, w_gate, w_up, w_down, routes, gates):
    groups = QH // KVH
    nblocks = TOKENS // TOK_DEV
    pad_rows = BACK * TOK_DEV
    window_rows = (BACK + 1) * TOK_DEV
    keys_pad = jnp.concatenate([jnp.zeros((pad_rows, KVH * DH), keys.dtype), keys], 0)
    values_pad = jnp.concatenate([jnp.zeros((pad_rows, KVH * DH), values.dtype), values], 0)
    scale = 1.0 / math.sqrt(DH)

    def attend(block_id):
        start = (block_id * TOK_DEV).astype(jnp.int32)
        query_block = lax.dynamic_slice_in_dim(queries, start, TOK_DEV, 0).astype(jnp.float32).reshape(TOK_DEV, KVH, groups, DH)
        key_block = lax.dynamic_slice_in_dim(keys_pad, start, window_rows, 0).astype(jnp.float32).reshape(window_rows, KVH, DH)
        value_block = lax.dynamic_slice_in_dim(values_pad, start, window_rows, 0).astype(jnp.float32).reshape(window_rows, KVH, DH)
        scores = jnp.einsum('tkgd,skd->kgts', query_block, key_block) * scale
        query_pos = start + jnp.arange(TOK_DEV, dtype=jnp.int32)
        key_pos = start - pad_rows + jnp.arange(window_rows, dtype=jnp.int32)
        allowed = (key_pos[None, :] >= 0) & (key_pos[None, :] <= query_pos[:, None])
        scores = jnp.where(allowed, scores, -jnp.inf)
        highest = lax.optimization_barrier(jnp.max(scores, -1, keepdims=True))
        expd = jnp.exp(scores - highest)
        weights = (expd / lax.optimization_barrier(jnp.sum(expd, -1, keepdims=True))).astype(jnp.bfloat16)
        mixed = jnp.einsum('kgts,skd->tkgd', weights.astype(jnp.float32), value_block)
        return mixed.astype(jnp.bfloat16).reshape(TOK_DEV, QH * DH)
    attended = lax.map(attend, jnp.arange(nblocks, dtype=jnp.int32)).reshape(TOKENS, QH * DH)
    stream = residual.astype(jnp.float32) + attended.astype(jnp.float32)
    mean_sq = lax.optimization_barrier(jnp.mean(stream * stream, -1, keepdims=True))
    normed = (stream * lax.rsqrt(mean_sq + 1e-06) * norm_gain).astype(jnp.bfloat16)
    capacity = 4 * TOK_DEV // EXPERTS
    per_expert = nblocks * capacity
    picks = routes.reshape(nblocks, 2 * TOK_DEV).astype(jnp.int32)
    one_hot = (picks[:, :, None] == jnp.arange(EXPERTS, dtype=jnp.int32)[None, None, :]).astype(jnp.int32)
    order_rank = lax.optimization_barrier(jnp.sum((jnp.cumsum(one_hot, 1) - 1) * one_hot, -1)).astype(jnp.int32)
    slot_index = (picks * per_expert + jnp.arange(nblocks, dtype=jnp.int32)[:, None] * capacity + order_rank).reshape(-1).astype(jnp.int32)
    token_of_pick = (jnp.arange(2 * TOKENS, dtype=jnp.int32) // 2).astype(jnp.int32)
    table = jnp.full((EXPERTS * per_expert,), TOKENS, jnp.int32).at[slot_index].set(token_of_pick)
    padded = jnp.concatenate([normed, jnp.zeros((1, D), normed.dtype)], 0)

    def run_expert(expert_id):
        rows = padded[lax.dynamic_slice_in_dim(table, (expert_id * per_expert).astype(jnp.int32), per_expert, 0)]
        return feed_forward(rows, w_gate[expert_id], w_up[expert_id], w_down[expert_id])
    expert_out = lax.map(run_expert, jnp.arange(EXPERTS, dtype=jnp.int32)).reshape(EXPERTS * per_expert, D)
    picked = expert_out[slot_index].astype(jnp.float32).reshape(TOKENS, 2, D)
    mixture = lax.optimization_barrier(jnp.sum(gates[:, :, None] * picked, 1))
    return (stream + mixture).astype(jnp.bfloat16)
```

```python
import functools
import math

import jax
import jax.numpy as jnp
from jax import lax
from jax.experimental import pallas as pl
from jax.experimental.pallas import tpu as pltpu
from jax.sharding import PartitionSpec as P

D = 1024
QH = 8
KVH = 4
DH = 128
BACK = 3


MESH = pl.DeviceIdType.MESH
PIECES = 4
SLABS = 4
STRIPS = 4
EARLY = 4


def layer_kernel(
    lanes, outers, query_ref, key_ref, value_ref, residual_ref, gain_ref, route_ref, pick_ref,
    gate_ref, up_ref, down_ref, out_ref,
    key_halo, value_halo, top, mass, stream, shares_ref, share_in, columns, far_gate, far_up, far_down,
    rows, acts, give, mate_in, back, back_in,
    halo_send, halo_recv, share_send, share_recv, cross_send, cross_recv, spread_send, spread_recv,
    row_send, row_recv, mate_send, mate_recv, give_send, give_recv, back_send, back_recv,
):
    outer, inner = lax.axis_index("outer"), lax.axis_index("inner")
    total = outers * lanes
    spots = lanes // 2
    near = spots // 2
    crew = 2 * near
    spot, core = inner // 2, inner % 2
    mate = 2 * spot + (1 - core)
    base = (spot // near) * near
    here = spot - base
    place_in_crew = inner - 2 * base
    partner = lax.rem(inner + lanes // 2, lanes)
    tok_rows, width = query_ref.shape
    hidden = gate_ref.shape[2]
    groups = QH // KVH
    place = outer * lanes + inner
    piece = tok_rows // PIECES
    wide_strip = width // STRIPS
    units = 2 * SLABS + STRIPS

    def at_piece(k):
        return pl.ds(pl.multiple_of(k * piece, piece), piece)

    def at_strip(k):
        return pl.ds(pl.multiple_of(k * wide_strip, wide_strip), wide_strip)

    def remote(src, dst, send, recv, to, at_outer=None):
        return pltpu.make_async_remote_copy(
            src_ref=src, dst_ref=dst, send_sem=send, recv_sem=recv,
            device_id={"outer": outer if at_outer is None else at_outer, "inner": to}, device_id_type=MESH,
        )

    def whole_id(to):
        return {"outer": to // lanes, "inner": lax.rem(to, lanes)}

    barrier = pltpu.get_barrier_semaphore()

    @pl.loop(1, crew)
    def _(step):
        to = 2 * base + lax.rem(place_in_crew + step, crew)
        pl.semaphore_signal(barrier, inc=1, device_id={"outer": outer, "inner": to}, device_id_type=MESH)

    pl.semaphore_signal(barrier, inc=1, device_id={"outer": outer, "inner": partner}, device_id_type=MESH)

    @pl.loop(1, outers)
    def _(step):
        to = lax.rem(outer + step, outers)
        pl.semaphore_signal(barrier, inc=1, device_id={"outer": to, "inner": inner}, device_id_type=MESH)

    expected = crew - 1 + 1 + outers - 1
    for shift in (-2, -1, 1, 2):
        other = place + shift
        reaches = (other >= 0) & (other < total)

        @pl.when(reaches)
        def _():
            pl.semaphore_signal(barrier, inc=1, device_id=whole_id(other), device_id_type=MESH)

        expected = expected + reaches.astype(jnp.int32)

    @pl.loop(0, crew)
    def _(member):
        for which in range(2):
            expert = lax.rem(2 * base + member + which * (lanes // 2), lanes)
            chosen = jnp.where(route_ref[...] == expert, pick_ref[...], 0.0)
            shares_ref[member, which] = jnp.sum(chosen, axis=0, keepdims=True)

    pl.semaphore_wait(barrier, expected)

    even = core == 0
    halos = ((key_ref, key_halo), (value_ref, value_halo))

    def halo_copy(kind, held, ahead, lane):
        own_ref, halo = halos[kind]
        src = own_ref if held == 0 else halo.at[held - 1]
        return pltpu.make_async_remote_copy(
            src_ref=src, dst_ref=halo.at[held + ahead - 1],
            send_sem=halo_send.at[kind, lane], recv_sem=halo_recv.at[kind, held + ahead - 1],
            device_id=whole_id(jnp.minimum(place + ahead, total - 1)), device_id_type=MESH,
        )

    goes_one = place + 1 < total
    goes_two = even & (place + 2 < total)
    plan = (
        (0, 1, goes_one),
        (0, 2, goes_two),
        (1, 1, even & (place >= 1)),
        (1, 2, goes_two & (place >= 1)),
        (2, 1, even & (place >= 2)),
    )

    def halo_start(kind, lane):
        held, ahead, active = plan[lane]

        @pl.when(active)
        def _():
            halo_copy(kind, held, ahead, lane).start()

    def halo_wait(kind, held):
        own_ref, halo = halos[kind]

        @pl.when(place >= held)
        def _():
            pltpu.make_async_remote_copy(
                src_ref=own_ref, dst_ref=halo.at[held - 1],
                send_sem=halo_send.at[kind, 0], recv_sem=halo_recv.at[kind, held - 1],
                device_id=whole_id(jnp.maximum(place - 1, 0)), device_id_type=MESH,
            ).wait_recv()

    def slab(unit, share, own):
        if unit < 2 * SLABS:
            depth = width // outers
            step = depth // SLABS
            at = pl.ds(pl.multiple_of(share * depth + (unit % SLABS) * step, step), step)
            if unit < SLABS:
                return gate_ref.at[0, at] if own else far_gate.at[at]
            return up_ref.at[0, at] if own else far_up.at[at]
        depth = hidden // outers
        at = pl.ds(pl.multiple_of(share * depth, depth), depth)
        strip = pl.ds((unit - 2 * SLABS) * wide_strip, wide_strip)
        return down_ref.at[0, at, strip] if own else far_down.at[at, strip]

    def cross_copy(unit):
        return remote(
            slab(unit, outer, True), slab(unit, outer, False), cross_send.at[unit], cross_recv.at[unit], partner
        )

    def spread_copy(unit, to):
        part = slab(unit, outer, False)
        return remote(part, part, spread_send.at[unit, to], spread_recv.at[unit, outer], inner, to)

    def spread(unit):
        cross_copy(unit).wait_recv()

        @pl.loop(1, outers)
        def _(step):
            spread_copy(unit, lax.rem(outer + step, outers)).start()

    def spread_wait(unit):
        @pl.loop(1, outers)
        def _(step):
            source = lax.rem(outer + step, outers)
            part = slab(unit, source, False)
            remote(
                part, part, spread_send.at[unit, source], spread_recv.at[unit, source], inner, source
            ).wait_recv()

    def share_copy(member, slot):
        return remote(
            shares_ref.at[member], share_in.at[slot], share_send.at[member], share_recv.at[slot], 2 * base + member
        )

    for lane in (1, 0):
        halo_start(0, lane)
    for lane in (1, 0):
        halo_start(1, lane)

    @pl.loop(1, crew)
    def _(step):
        share_copy(lax.rem(place_in_crew + step, crew), place_in_crew).start()

    share_in[place_in_crew] = shares_ref[place_in_crew]

    def attend(held):
        @pl.loop(0, KVH)
        def _(head):
            wide = pl.ds(pl.multiple_of(head * groups * DH, groups * DH), groups * DH)
            narrow = pl.ds(pl.multiple_of(head * DH, DH), DH)
            asked = query_ref[:, wide]
            if held == 0:
                keys, vals = key_ref[:, narrow], value_ref[:, narrow]
            else:
                keys, vals = key_halo[held - 1, :, narrow], value_halo[held - 1, :, narrow]
            mixed = []
            for group in range(groups):
                scores = lax.dot_general(
                    asked[:, group * DH : (group + 1) * DH], keys, (((1,), (1,)), ((), ())),
                    preferred_element_type=jnp.float32,
                ) * (1.0 / math.sqrt(DH))
                if held == 0:
                    row_id = lax.broadcasted_iota(jnp.int32, scores.shape, 0)
                    col_id = lax.broadcasted_iota(jnp.int32, scores.shape, 1)
                    scores = jnp.where(col_id <= row_id, scores, -jnp.inf)
                highest = jnp.max(scores, -1, keepdims=True)
                slot = head * groups + group
                if held:
                    highest = jnp.maximum(top[slot], highest)
                expd = jnp.exp(scores - highest)
                summed = jnp.sum(expd, -1, keepdims=True)
                part = jnp.dot(expd.astype(jnp.bfloat16), vals, preferred_element_type=jnp.float32)
                if held:
                    keep = jnp.exp(top[slot] - highest)
                    summed = summed + mass[slot] * keep
                    at = pl.ds(pl.multiple_of(slot * DH, DH), DH)
                    part = part + stream[:, at] * keep
                top[slot] = highest
                mass[slot] = summed
                mixed.append(part)
            stream[:, wide] = jnp.concatenate(mixed, 1)

    attend(0)
    for kind in range(2):
        halo_wait(kind, 1)
        halo_start(kind, 3)
        halo_start(kind, 2)
        halo_wait(kind, 2)
        halo_start(kind, 4)

    edge = (spot == 0) | (spot == spots - 1)
    for unit in range(EARLY):
        cross_copy(unit).start()

    @pl.when(jnp.logical_not(edge))
    def _():
        for unit in range(EARLY, units):
            cross_copy(unit).start()

    @pl.loop(1, crew)
    def _(step):
        source = lax.rem(place_in_crew + step, crew)
        share_copy(source, source).wait_recv()

    @pl.loop(0, crew)
    def _(member):
        row_id = lax.broadcasted_iota(jnp.int32, (tok_rows, tok_rows), 0)
        col_id = lax.broadcasted_iota(jnp.int32, (tok_rows, tok_rows), 1)
        for which in range(2):
            share = jnp.broadcast_to(share_in[member, which], (tok_rows, tok_rows))
            columns[member, which] = jnp.sum(jnp.where(row_id == col_id, share, 0.0), axis=1, keepdims=True)

    for held in range(1, BACK + 1):
        if held == BACK:
            halo_wait(0, held)
            halo_wait(1, held)

        @pl.when(place >= held)
        def _():
            attend(held)

    @pl.loop(0, QH)
    def _(slot):
        at = pl.ds(pl.multiple_of(slot * DH, DH), DH)
        attended = (stream[:, at] / mass[slot]).astype(jnp.bfloat16).astype(jnp.float32)
        stream[:, at] = residual_ref[:, at].astype(jnp.float32) + attended

    def row_copy(chip, k, to):
        part = rows.at[chip, core, at_piece(k)]
        return remote(part, part, row_send.at[to, k], row_recv.at[chip, k], 2 * (base + to) + core)

    def mate_copy(chip, k):
        part = rows.at[chip, core, at_piece(k)]
        return remote(part, part, mate_send.at[chip, k], mate_recv.at[chip, k], mate)

    others = [lax.rem(here + step, near) for step in range(1, near)]

    for k in range(PIECES):
        at = pl.ds(k * piece, piece)
        kept = stream[at, :]
        mean_sq = jnp.mean(kept * kept, -1, keepdims=True)
        rows[here, core, at] = (kept * lax.rsqrt(mean_sq + 1e-06) * gain_ref[...]).astype(jnp.bfloat16)
        for chip in others:
            row_copy(here, k, chip).start()
        mate_copy(here, k).start()

    @pl.when(edge)
    def _():
        for unit in range(EARLY, units):
            cross_copy(unit).start()

    def hide(chip, k, which):
        at = at_piece(k)
        block = jnp.concatenate([rows[chip, side, at] for side in range(2)], 0)
        gates, ups = (far_gate, far_up) if which else (gate_ref.at[0], up_ref.at[0])
        gate_part = jnp.dot(block, gates[...], preferred_element_type=jnp.float32)
        up_part = jnp.dot(block, ups[...], preferred_element_type=jnp.float32)
        act = (gate_part / (1.0 + jnp.exp(-gate_part)) * up_part).astype(jnp.bfloat16)
        for side in range(2):
            acts[which, chip, side, at] = act[side * piece : (side + 1) * piece]

    for unit in range(EARLY):
        spread(unit)
    for k in range(PIECES):
        mate_copy(here, k).wait_recv()

    @pl.loop(0, PIECES)
    def _(k):
        hide(here, k, 0)

    for k in range(PIECES):
        for chip in others:
            row_copy(chip, k, here).wait_recv()
            mate_copy(chip, k).start()
        if EARLY + k < 2 * SLABS:
            spread(EARLY + k)
    for chip in others:
        for k in range(PIECES):
            mate_copy(chip, k).wait_recv()

        @pl.loop(0, PIECES)
        def _(k):
            hide(chip, k, 0)

    for unit in range(2 * SLABS):
        spread_wait(unit)
    spread(2 * SLABS)

    for chip in others + [here]:

        @pl.loop(0, PIECES)
        def _(k):
            hide(chip, k, 1)

    def give_copy(chip, strip):
        at = at_strip(strip)
        return remote(
            give.at[chip, :, at], mate_in.at[chip, :, at],
            give_send.at[chip, strip], give_recv.at[chip, strip], mate,
        )

    def back_copy(chip, slot, strip):
        at = at_strip(strip)
        return remote(
            back.at[chip, :, at], back_in.at[slot, :, at],
            back_send.at[chip, strip], back_recv.at[slot, strip], 2 * (base + chip) + core,
        )

    def part_of(chip, side, strip):
        at = at_strip(strip)
        out = None
        for which in range(2):
            downs = far_down[:, at] if which else down_ref[0, :, at]
            mine = jnp.dot(acts[which, chip, side], downs, preferred_element_type=jnp.float32)
            mine = mine.astype(jnp.bfloat16).astype(jnp.float32) * columns[2 * chip + side, which]
            out = mine if out is None else out + mine
        return out

    for strip in range(STRIPS):
        if strip + 1 < STRIPS:
            spread(2 * SLABS + strip + 1)
        spread_wait(2 * SLABS + strip)
        at = at_strip(strip)
        for chip in others + [here]:
            give[chip, :, at] = part_of(chip, 1 - core, strip).astype(jnp.bfloat16)
            give_copy(chip, strip).start()
        for chip in others:
            mine = part_of(chip, core, strip)
            give_copy(chip, strip).wait_recv()
            back[chip, :, at] = (mine + mate_in[chip, :, at].astype(jnp.float32)).astype(jnp.bfloat16)
            back_copy(chip, here, strip).start()
        mine = part_of(here, core, strip)
        give_copy(here, strip).wait_recv()
        stream[:, at] = stream[:, at] + (mine + mate_in[here, :, at].astype(jnp.float32))

    @pl.loop(1, crew)
    def _(step):
        share_copy(lax.rem(place_in_crew + step, crew), place_in_crew).wait_send()

    for kind in range(2):
        for lane, (held, ahead, active) in enumerate(plan):

            @pl.when(active)
            def _():
                halo_copy(kind, held, ahead, lane).wait_send()

    for unit in range(units):
        cross_copy(unit).wait_send()

        @pl.loop(1, outers)
        def _(step):
            spread_copy(unit, lax.rem(outer + step, outers)).wait_send()

    for k in range(PIECES):
        for chip in others:
            row_copy(here, k, chip).wait_send()
            mate_copy(chip, k).wait_send()
        mate_copy(here, k).wait_send()

    for strip in range(STRIPS):
        at = at_strip(strip)
        done = stream[:, at]
        for chip in others:
            back_copy(here, chip, strip).wait_recv()
            done = done + back_in[chip, :, at].astype(jnp.float32)
        out_ref[:, at] = done.astype(jnp.bfloat16)

    for strip in range(STRIPS):
        for chip in others:
            back_copy(chip, here, strip).wait_send()
        for chip in others + [here]:
            give_copy(chip, strip).wait_send()


def local(lanes, outers, queries, keys, values, residual, norm_gain, w_gate, w_up, w_down, routes, gates):
    tok_rows, width = queries.shape
    hidden = w_gate.shape[2]
    near = lanes // 4
    crew = 2 * near
    units = 2 * SLABS + STRIPS
    vmem = pl.BlockSpec(memory_space=pltpu.VMEM)
    dma = pltpu.SemaphoreType.DMA
    block = (tok_rows, width)
    return pl.pallas_call(
        functools.partial(layer_kernel, lanes, outers),
        out_shape=jax.ShapeDtypeStruct(block, jnp.bfloat16),
        in_specs=[vmem] * 10,
        out_specs=vmem,
        scratch_shapes=[
            pltpu.VMEM((BACK,) + keys.shape, jnp.bfloat16),
            pltpu.VMEM((BACK,) + values.shape, jnp.bfloat16),
            pltpu.VMEM((QH, tok_rows, 1), jnp.float32),
            pltpu.VMEM((QH, tok_rows, 1), jnp.float32),
            pltpu.VMEM(block, jnp.float32),
            pltpu.VMEM((crew, 2, 1, tok_rows), jnp.float32),
            pltpu.VMEM((crew, 2, 1, tok_rows), jnp.float32),
            pltpu.VMEM((crew, 2, tok_rows, 1), jnp.float32),
            pltpu.VMEM((width, hidden), jnp.bfloat16),
            pltpu.VMEM((width, hidden), jnp.bfloat16),
            pltpu.VMEM((hidden, width), jnp.bfloat16),
            pltpu.VMEM((near, 2) + block, jnp.bfloat16),
            pltpu.VMEM((2, near, 2, tok_rows, hidden), jnp.bfloat16),
            pltpu.VMEM((near,) + block, jnp.bfloat16),
            pltpu.VMEM((near,) + block, jnp.bfloat16),
            pltpu.VMEM((near,) + block, jnp.bfloat16),
            pltpu.VMEM((near,) + block, jnp.bfloat16),
            dma((2, 5)), dma((2, BACK)),
            dma((crew,)), dma((crew,)),
            dma((units,)), dma((units,)),
            dma((units, outers)), dma((units, outers)),
            dma((near, PIECES)), dma((near, PIECES)),
            dma((near, PIECES)), dma((near, PIECES)),
            dma((near, STRIPS)), dma((near, STRIPS)),
            dma((near, STRIPS)), dma((near, STRIPS)),
        ],
        compiler_params=pltpu.CompilerParams(
            collective_id=0, has_side_effects=True, vmem_limit_bytes=60 * 1024 * 1024
        ),
    )(queries, keys, values, residual, norm_gain[None, :], routes.T, gates.T, w_gate, w_up, w_down)


def solution(mesh):
    return jax.shard_map(
        functools.partial(local, mesh.shape["inner"], mesh.shape["outer"]),
        mesh=mesh,
        in_specs=(
            P(("outer", "inner"), None),
            P(("outer", "inner"), None),
            P(("outer", "inner"), None),
            P(("outer", "inner"), None),
            P(),
            P("inner", None, None),
            P("inner", None, None),
            P("inner", None, None),
            P(("outer", "inner"), None),
            P(("outer", "inner"), None),
        ),
        out_specs=P(("outer", "inner"), None),
        check_vma=False,
    )
```

```python
import functools
import math

import jax
import jax.numpy as jnp
from jax import lax
from jax.experimental import pallas as pl
from jax.experimental.pallas import tpu as pltpu
from jax.sharding import PartitionSpec as P

D = 1024
QH = 8
KVH = 4
DH = 128
BACK = 3


MESH = pl.DeviceIdType.MESH
PIECES = 4
SLABS = 4
STRIPS = 4
INNER = 8
LAG = 2
FIRST = 0
MID = 0
EARLY = 8


def layer_kernel(
    lanes, outers, query_ref, key_ref, value_ref, residual_ref, gain_ref, route_ref, pick_ref,
    gate_ref, up_ref, down_ref, out_ref,
    key_halo, value_halo, top, mass, stream, shares_ref, share_in, columns, far_gate, far_up, far_down,
    rows, acts, give, mate_in, back, back_in,
    halo_send, halo_recv, share_send, share_recv, cross_send, cross_recv, spread_send, spread_recv,
    row_send, row_recv, mate_send, mate_recv, give_send, give_recv, back_send, back_recv,
):
    outer, inner = lax.axis_index("outer"), lax.axis_index("inner")
    total = outers * lanes
    spots = lanes // 2
    near = spots // 2
    crew = 2 * near
    spot, core = inner // 2, inner % 2
    mate = 2 * spot + (1 - core)
    base = (spot // near) * near
    here = spot - base
    place_in_crew = inner - 2 * base
    partner = lax.rem(inner + lanes // 2, lanes)
    tok_rows, width = query_ref.shape
    hidden = gate_ref.shape[2]
    groups = QH // KVH
    place = outer * lanes + inner
    piece = tok_rows // PIECES
    wide_strip = width // STRIPS
    units = 2 * SLABS + STRIPS

    def at_piece(k):
        return pl.ds(pl.multiple_of(k * piece, piece), piece)

    def at_strip(k):
        return pl.ds(pl.multiple_of(k * wide_strip, wide_strip), wide_strip)

    def remote(src, dst, send, recv, to, at_outer=None):
        return pltpu.make_async_remote_copy(
            src_ref=src, dst_ref=dst, send_sem=send, recv_sem=recv,
            device_id={"outer": outer if at_outer is None else at_outer, "inner": to}, device_id_type=MESH,
        )

    def whole_id(to):
        return {"outer": to // lanes, "inner": lax.rem(to, lanes)}

    barrier = pltpu.get_barrier_semaphore()

    @pl.loop(1, crew)
    def _(step):
        to = 2 * base + lax.rem(place_in_crew + step, crew)
        pl.semaphore_signal(barrier, inc=1, device_id={"outer": outer, "inner": to}, device_id_type=MESH)

    pl.semaphore_signal(barrier, inc=1, device_id={"outer": outer, "inner": partner}, device_id_type=MESH)

    @pl.loop(1, outers)
    def _(step):
        to = lax.rem(outer + step, outers)
        pl.semaphore_signal(barrier, inc=1, device_id={"outer": to, "inner": inner}, device_id_type=MESH)

    expected = crew - 1 + 1 + outers - 1
    for shift in (-2, -1, 1, 2):
        other = place + shift
        reaches = (other >= 0) & (other < total)

        @pl.when(reaches)
        def _():
            pl.semaphore_signal(barrier, inc=1, device_id=whole_id(other), device_id_type=MESH)

        expected = expected + reaches.astype(jnp.int32)

    @pl.loop(0, crew)
    def _(member):
        for which in range(2):
            expert = lax.rem(2 * base + member + which * (lanes // 2), lanes)
            chosen = jnp.where(route_ref[...] == expert, pick_ref[...], 0.0)
            shares_ref[member, which] = jnp.sum(chosen, axis=0, keepdims=True)

    pl.semaphore_wait(barrier, expected)

    even = core == 0
    halos = ((key_ref, key_halo), (value_ref, value_halo))

    def halo_copy(kind, held, ahead, lane):
        own_ref, halo = halos[kind]
        src = own_ref if held == 0 else halo.at[held - 1]
        return pltpu.make_async_remote_copy(
            src_ref=src, dst_ref=halo.at[held + ahead - 1],
            send_sem=halo_send.at[kind, lane], recv_sem=halo_recv.at[kind, held + ahead - 1],
            device_id=whole_id(jnp.minimum(place + ahead, total - 1)), device_id_type=MESH,
        )

    goes_one = place + 1 < total
    goes_two = even & (place + 2 < total)
    plan = (
        (0, 1, goes_one),
        (0, 2, goes_two),
        (1, 1, even & (place >= 1)),
        (1, 2, goes_two & (place >= 1)),
        (2, 1, even & (place >= 2)),
    )

    def halo_start(kind, lane):
        held, ahead, active = plan[lane]

        @pl.when(active)
        def _():
            halo_copy(kind, held, ahead, lane).start()

    def halo_wait(kind, held):
        own_ref, halo = halos[kind]

        @pl.when(place >= held)
        def _():
            pltpu.make_async_remote_copy(
                src_ref=own_ref, dst_ref=halo.at[held - 1],
                send_sem=halo_send.at[kind, 0], recv_sem=halo_recv.at[kind, held - 1],
                device_id=whole_id(jnp.maximum(place - 1, 0)), device_id_type=MESH,
            ).wait_recv()

    edge = (spot == 0) | (spot == spots - 1)
    idle = place < BACK - 1
    def slab(unit, share, own):
        if unit < 2 * SLABS:
            depth = width // outers
            step = depth // SLABS
            at = pl.ds(pl.multiple_of(share * depth + (unit % SLABS) * step, step), step)
            if unit < SLABS:
                return gate_ref.at[0, at] if own else far_gate.at[at]
            return up_ref.at[0, at] if own else far_up.at[at]
        depth = hidden // outers
        at = pl.ds(pl.multiple_of(share * depth, depth), depth)
        strip = pl.ds((unit - 2 * SLABS) * wide_strip, wide_strip)
        return down_ref.at[0, at, strip] if own else far_down.at[at, strip]

    def cross_copy(unit):
        return remote(
            slab(unit, outer, True), slab(unit, outer, False), cross_send.at[unit], cross_recv.at[unit], partner
        )

    side = math.isqrt(outers)
    side = 1
    deep = outers // side
    row, column = outer // deep, lax.rem(outer, deep)

    def peer(down, along):
        return lax.rem(row + down, side) * deep + lax.rem(column + along, deep)

    def spread_copy(unit, share, to, lane):
        part = slab(unit, share, False)
        return remote(part, part, spread_send.at[unit, lane], spread_recv.at[unit, share], inner, to)

    neighbours = [(down, 0) for down in range(1, side)] + [(0, along) for along in range(1, deep)]

    def relays(unit):
        for down in range(1, side):
            for along in range(1, deep):
                first, then = ((0, along), (down, 0)) if unit % 2 else ((down, 0), (0, along))
                yield peer(*first), peer(*then), outers + down * deep + along

    def relay_sources(unit):
        return [(0, along) for along in range(1, deep)] if unit % 2 else [(down, 0) for down in range(1, side)]

    def share_wait(unit, share):
        spread_copy(unit, share, share, 0).wait_recv()

    def relay(unit):
        if side > 1 and deep > 1:
            for spot_of in relay_sources(unit):
                share_wait(unit, peer(*spot_of))
        for share, to, lane in relays(unit):
            spread_copy(unit, share, to, lane).start()

    def spread(unit):
        cross_copy(unit).wait_recv()
        for lane, spot_of in enumerate(neighbours):
            spread_copy(unit, outer, peer(*spot_of), lane).start()
        if unit >= LAG:
            relay(unit - LAG)

    def spread_unless_idle(unit):
        if unit:
            spread(unit)
        else:
            pl.when(jnp.logical_not(idle))(lambda: spread(unit))

    def spread_wait(unit):
        sources = relay_sources(unit) if side > 1 and deep > 1 else []
        for down in range(side):
            for along in range(deep):
                if (down or along) and (down, along) not in sources:
                    share_wait(unit, peer(down, along))

    def spread_sent(unit):
        for lane, spot_of in enumerate(neighbours):
            spread_copy(unit, outer, peer(*spot_of), lane).wait_send()
        for share, to, lane in relays(unit):
            spread_copy(unit, share, to, lane).wait_send()

    def share_copy(member, slot):
        return remote(
            shares_ref.at[member], share_in.at[slot], share_send.at[member], share_recv.at[slot], 2 * base + member
        )

    def cross_start(low, high):
        for unit in range(low, high):
            cross_copy(unit).start()

    pl.when(jnp.logical_not(idle))(lambda: cross_start(0, FIRST))
    for lane in (1, 0):
        halo_start(0, lane)
    for lane in (1, 0):
        halo_start(1, lane)

    @pl.loop(1, crew)
    def _(step):
        share_copy(lax.rem(place_in_crew + step, crew), place_in_crew).start()

    share_in[place_in_crew] = shares_ref[place_in_crew]

    def attend(held):
        @pl.loop(0, KVH)
        def _(head):
            wide = pl.ds(pl.multiple_of(head * groups * DH, groups * DH), groups * DH)
            narrow = pl.ds(pl.multiple_of(head * DH, DH), DH)
            asked = query_ref[:, wide]
            if held == 0:
                keys, vals = key_ref[:, narrow], value_ref[:, narrow]
            else:
                keys, vals = key_halo[held - 1, :, narrow], value_halo[held - 1, :, narrow]
            mixed = []
            for group in range(groups):
                scores = lax.dot_general(
                    asked[:, group * DH : (group + 1) * DH], keys, (((1,), (1,)), ((), ())),
                    preferred_element_type=jnp.float32,
                ) * (1.0 / math.sqrt(DH))
                if held == 0:
                    row_id = lax.broadcasted_iota(jnp.int32, scores.shape, 0)
                    col_id = lax.broadcasted_iota(jnp.int32, scores.shape, 1)
                    scores = jnp.where(col_id <= row_id, scores, -jnp.inf)
                highest = jnp.max(scores, -1, keepdims=True)
                slot = head * groups + group
                if held:
                    highest = jnp.maximum(top[slot], highest)
                expd = jnp.exp(scores - highest)
                summed = jnp.sum(expd, -1, keepdims=True)
                part = jnp.dot(expd.astype(jnp.bfloat16), vals, preferred_element_type=jnp.float32)
                if held:
                    keep = jnp.exp(top[slot] - highest)
                    summed = summed + mass[slot] * keep
                    at = pl.ds(pl.multiple_of(slot * DH, DH), DH)
                    part = part + stream[:, at] * keep
                top[slot] = highest
                mass[slot] = summed
                mixed.append(part)
            stream[:, wide] = jnp.concatenate(mixed, 1)

    attend(0)
    for kind in range(2):
        halo_wait(kind, 1)
        halo_start(kind, 3)
        halo_start(kind, 2)
        halo_wait(kind, 2)
        halo_start(kind, 4)

    pl.when(jnp.logical_not(edge))(lambda: cross_start(FIRST, INNER))

    @pl.loop(1, crew)
    def _(step):
        source = lax.rem(place_in_crew + step, crew)
        share_copy(source, source).wait_recv()

    @pl.loop(0, crew)
    def _(member):
        row_id = lax.broadcasted_iota(jnp.int32, (tok_rows, tok_rows), 0)
        col_id = lax.broadcasted_iota(jnp.int32, (tok_rows, tok_rows), 1)
        for which in range(2):
            share = jnp.broadcast_to(share_in[member, which], (tok_rows, tok_rows))
            columns[member, which] = jnp.sum(jnp.where(row_id == col_id, share, 0.0), axis=1, keepdims=True)

    for held in range(1, BACK + 1):
        if held == BACK:
            @pl.when(idle)
            def _():
                spread(0)
                cross_start(0, FIRST)

            pl.when(edge)(lambda: cross_start(FIRST, EARLY))
            for unit in range(MID):
                spread_unless_idle(unit)
            halo_wait(0, held)
            halo_wait(1, held)

        @pl.when(place >= held)
        def _():
            attend(held)

    @pl.loop(0, QH)
    def _(slot):
        at = pl.ds(pl.multiple_of(slot * DH, DH), DH)
        attended = (stream[:, at] / mass[slot]).astype(jnp.bfloat16).astype(jnp.float32)
        stream[:, at] = residual_ref[:, at].astype(jnp.float32) + attended

    def row_copy(chip, k, to):
        part = rows.at[chip, core, at_piece(k)]
        return remote(part, part, row_send.at[to, k], row_recv.at[chip, k], 2 * (base + to) + core)

    def mate_copy(chip, k):
        part = rows.at[chip, core, at_piece(k)]
        return remote(part, part, mate_send.at[chip, k], mate_recv.at[chip, k], mate)

    others = [lax.rem(here + step, near) for step in range(1, near)]

    for k in range(PIECES):
        at = pl.ds(k * piece, piece)
        kept = stream[at, :]
        mean_sq = jnp.mean(kept * kept, -1, keepdims=True)
        rows[here, core, at] = (kept * lax.rsqrt(mean_sq + 1e-06) * gain_ref[...]).astype(jnp.bfloat16)
        for chip in others:
            row_copy(here, k, chip).start()
        mate_copy(here, k).start()

    pl.when(edge)(lambda: cross_start(EARLY, units))
    pl.when(jnp.logical_not(edge))(lambda: cross_start(INNER, units))

    def hide(chip, k, which):
        at = at_piece(k)
        block = jnp.concatenate([rows[chip, side, at] for side in range(2)], 0)
        gates, ups = (far_gate, far_up) if which else (gate_ref.at[0], up_ref.at[0])
        gate_part = jnp.dot(block, gates[...], preferred_element_type=jnp.float32)
        up_part = jnp.dot(block, ups[...], preferred_element_type=jnp.float32)
        act = (gate_part / (1.0 + jnp.exp(-gate_part)) * up_part).astype(jnp.bfloat16)
        for side in range(2):
            acts[which, chip, side, at] = act[side * piece : (side + 1) * piece]

    for unit in range(MID, 4):
        spread_unless_idle(unit)
    for k in range(PIECES):
        mate_copy(here, k).wait_recv()

    @pl.loop(0, PIECES // 2)
    def _(k):
        hide(here, k, 0)

    spread(4)

    @pl.loop(PIECES // 2, PIECES)
    def _(k):
        hide(here, k, 0)

    for unit in range(5, 2 * SLABS):
        spread(unit)
    for k in range(PIECES):
        for chip in others:
            row_copy(chip, k, here).wait_recv()
            mate_copy(chip, k).start()
    for unit in range(2 * SLABS, 2 * SLABS + LAG):
        spread(unit)
    for chip in others:
        for k in range(PIECES):
            mate_copy(chip, k).wait_recv()

        @pl.loop(0, PIECES)
        def _(k):
            hide(chip, k, 0)

    for unit in range(2 * SLABS):
        spread_wait(unit)

    rest = list(range(2 * SLABS + LAG, units))
    for chip in others + [here]:

        @pl.loop(0, PIECES)
        def _(k):
            hide(chip, k, 1)

        if rest:
            spread(rest.pop(0))

    for unit in rest:
        spread(unit)
    for unit in range(units - LAG, units):
        relay(unit)

    def give_copy(chip, strip):
        at = at_strip(strip)
        return remote(
            give.at[chip, :, at], mate_in.at[chip, :, at],
            give_send.at[chip, strip], give_recv.at[chip, strip], mate,
        )

    def back_copy(chip, slot, strip):
        at = at_strip(strip)
        return remote(
            back.at[chip, :, at], back_in.at[slot, :, at],
            back_send.at[chip, strip], back_recv.at[slot, strip], 2 * (base + chip) + core,
        )

    def part_of(chip, side, strip):
        at = at_strip(strip)
        out = None
        for which in range(2):
            downs = far_down[:, at] if which else down_ref[0, :, at]
            mine = jnp.dot(acts[which, chip, side], downs, preferred_element_type=jnp.float32)
            mine = mine.astype(jnp.bfloat16).astype(jnp.float32) * columns[2 * chip + side, which]
            out = mine if out is None else out + mine
        return out

    for strip in range(STRIPS):
        spread_wait(2 * SLABS + strip)
        at = at_strip(strip)
        for chip in others + [here]:
            give[chip, :, at] = part_of(chip, 1 - core, strip).astype(jnp.bfloat16)
            give_copy(chip, strip).start()
        for chip in others:
            mine = part_of(chip, core, strip)
            give_copy(chip, strip).wait_recv()
            back[chip, :, at] = (mine + mate_in[chip, :, at].astype(jnp.float32)).astype(jnp.bfloat16)
            back_copy(chip, here, strip).start()
        mine = part_of(here, core, strip)
        give_copy(here, strip).wait_recv()
        stream[:, at] = stream[:, at] + (mine + mate_in[here, :, at].astype(jnp.float32))

    @pl.loop(1, crew)
    def _(step):
        share_copy(lax.rem(place_in_crew + step, crew), place_in_crew).wait_send()

    for kind in range(2):
        for lane, (held, ahead, active) in enumerate(plan):

            @pl.when(active)
            def _():
                halo_copy(kind, held, ahead, lane).wait_send()

    for unit in range(units):
        cross_copy(unit).wait_send()
        spread_sent(unit)

    for k in range(PIECES):
        for chip in others:
            row_copy(here, k, chip).wait_send()
            mate_copy(chip, k).wait_send()
        mate_copy(here, k).wait_send()

    for strip in range(STRIPS):
        at = at_strip(strip)
        done = stream[:, at]
        for chip in others:
            back_copy(here, chip, strip).wait_recv()
            done = done + back_in[chip, :, at].astype(jnp.float32)
        out_ref[:, at] = done.astype(jnp.bfloat16)

    for strip in range(STRIPS):
        for chip in others:
            back_copy(chip, here, strip).wait_send()
        for chip in others + [here]:
            give_copy(chip, strip).wait_send()


def local(lanes, outers, queries, keys, values, residual, norm_gain, w_gate, w_up, w_down, routes, gates):
    tok_rows, width = queries.shape
    hidden = w_gate.shape[2]
    near = lanes // 4
    crew = 2 * near
    units = 2 * SLABS + STRIPS
    vmem = pl.BlockSpec(memory_space=pltpu.VMEM)
    dma = pltpu.SemaphoreType.DMA
    block = (tok_rows, width)
    return pl.pallas_call(
        functools.partial(layer_kernel, lanes, outers),
        out_shape=jax.ShapeDtypeStruct(block, jnp.bfloat16),
        in_specs=[vmem] * 10,
        out_specs=vmem,
        scratch_shapes=[
            pltpu.VMEM((BACK,) + keys.shape, jnp.bfloat16),
            pltpu.VMEM((BACK,) + values.shape, jnp.bfloat16),
            pltpu.VMEM((QH, tok_rows, 1), jnp.float32),
            pltpu.VMEM((QH, tok_rows, 1), jnp.float32),
            pltpu.VMEM(block, jnp.float32),
            pltpu.VMEM((crew, 2, 1, tok_rows), jnp.float32),
            pltpu.VMEM((crew, 2, 1, tok_rows), jnp.float32),
            pltpu.VMEM((crew, 2, tok_rows, 1), jnp.float32),
            pltpu.VMEM((width, hidden), jnp.bfloat16),
            pltpu.VMEM((width, hidden), jnp.bfloat16),
            pltpu.VMEM((hidden, width), jnp.bfloat16),
            pltpu.VMEM((near, 2) + block, jnp.bfloat16),
            pltpu.VMEM((2, near, 2, tok_rows, hidden), jnp.bfloat16),
            pltpu.VMEM((near,) + block, jnp.bfloat16),
            pltpu.VMEM((near,) + block, jnp.bfloat16),
            pltpu.VMEM((near,) + block, jnp.bfloat16),
            pltpu.VMEM((near,) + block, jnp.bfloat16),
            dma((2, 5)), dma((2, BACK)),
            dma((crew,)), dma((crew,)),
            dma((units,)), dma((units,)),
            dma((units, 2 * outers)), dma((units, outers)),
            dma((near, PIECES)), dma((near, PIECES)),
            dma((near, PIECES)), dma((near, PIECES)),
            dma((near, STRIPS)), dma((near, STRIPS)),
            dma((near, STRIPS)), dma((near, STRIPS)),
        ],
        compiler_params=pltpu.CompilerParams(
            collective_id=0, has_side_effects=True, vmem_limit_bytes=60 * 1024 * 1024
        ),
    )(queries, keys, values, residual, norm_gain[None, :], routes.T, gates.T, w_gate, w_up, w_down)


def solution(mesh):
    return jax.shard_map(
        functools.partial(local, mesh.shape["inner"], mesh.shape["outer"]),
        mesh=mesh,
        in_specs=(
            P(("outer", "inner"), None),
            P(("outer", "inner"), None),
            P(("outer", "inner"), None),
            P(("outer", "inner"), None),
            P(),
            P("inner", None, None),
            P("inner", None, None),
            P("inner", None, None),
            P(("outer", "inner"), None),
            P(("outer", "inner"), None),
        ),
        out_specs=P(("outer", "inner"), None),
        check_vma=False,
    )
```

```python
import functools
import math

import jax
import jax.numpy as jnp
from jax import lax
from jax.experimental import pallas as pl
from jax.experimental.pallas import tpu as pltpu
from jax.sharding import PartitionSpec as P

D = 1024
QH = 8
KVH = 4
DH = 128
BACK = 3


MESH = pl.DeviceIdType.MESH
PIECES = 4
HALVES = 2
EDGE_PACE = (0, 0, 8, 8)
INNER_PACE = (8, 8, 8, 8)
FORWARDS = (0, 0)
SLABS = 4
STRIPS = 4


def layer_kernel(
    lanes, outers, query_ref, key_ref, value_ref, residual_ref, gain_ref, route_ref, pick_ref,
    gate_ref, up_ref, down_ref, out_ref,
    key_halo, value_halo, top, mixed, stream, shares_ref, share_in, columns, far_gate, far_up, far_down,
    rows, acts, give, mate_in, back, back_in,
    halo_send, halo_recv, share_send, share_recv, cross_send, cross_recv, spread_send, spread_recv,
    row_send, row_recv, mate_send, mate_recv, give_send, give_recv, back_send, back_recv,
):
    outer, inner = lax.axis_index("outer"), lax.axis_index("inner")
    total = outers * lanes
    spots = lanes // 2
    near = spots // 2
    crew = 2 * near
    spot, core = inner // 2, inner % 2
    mate = 2 * spot + (1 - core)
    base = (spot // near) * near
    here = spot - base
    place_in_crew = inner - 2 * base
    partner = lax.rem(inner + lanes // 2, lanes)
    tok_rows, width = query_ref.shape
    hidden = gate_ref.shape[2]
    groups = QH // KVH
    place = outer * lanes + inner
    piece = tok_rows // PIECES
    wide_strip = width // STRIPS
    units = 2 * SLABS + STRIPS

    def at_piece(k):
        return pl.ds(pl.multiple_of(k * piece, piece), piece)

    def at_strip(k):
        return pl.ds(pl.multiple_of(k * wide_strip, wide_strip), wide_strip)

    def remote(src, dst, send, recv, to, at_outer=None):
        return pltpu.make_async_remote_copy(
            src_ref=src, dst_ref=dst, send_sem=send, recv_sem=recv,
            device_id={"outer": outer if at_outer is None else at_outer, "inner": to}, device_id_type=MESH,
        )

    def whole_id(to):
        return {"outer": to // lanes, "inner": lax.rem(to, lanes)}

    barrier = pltpu.get_barrier_semaphore()

    @pl.loop(1, crew)
    def _(step):
        to = 2 * base + lax.rem(place_in_crew + step, crew)
        pl.semaphore_signal(barrier, inc=1, device_id={"outer": outer, "inner": to}, device_id_type=MESH)

    pl.semaphore_signal(barrier, inc=1, device_id={"outer": outer, "inner": partner}, device_id_type=MESH)

    @pl.loop(1, outers)
    def _(step):
        to = lax.rem(outer + step, outers)
        pl.semaphore_signal(barrier, inc=1, device_id={"outer": to, "inner": inner}, device_id_type=MESH)

    expected = crew - 1 + 1 + outers - 1
    for shift in (-2, -1, 1, 2):
        other = place + shift
        reaches = (other >= 0) & (other < total)

        @pl.when(reaches)
        def _():
            pl.semaphore_signal(barrier, inc=1, device_id=whole_id(other), device_id_type=MESH)

        expected = expected + reaches.astype(jnp.int32)

    @pl.loop(0, crew)
    def _(member):
        for which in range(2):
            expert = lax.rem(2 * base + member + which * (lanes // 2), lanes)
            chosen = jnp.where(route_ref[...] == expert, pick_ref[...], 0.0)
            shares_ref[member, which] = jnp.sum(chosen, axis=0, keepdims=True)

    pl.semaphore_wait(barrier, expected)

    even = core == 0
    halos = ((key_ref, key_halo), (value_ref, value_halo))

    def halo_copy(kind, held, ahead, lane):
        own_ref, halo = halos[kind]
        src = own_ref if held == 0 else halo.at[held - 1]
        return pltpu.make_async_remote_copy(
            src_ref=src, dst_ref=halo.at[held + ahead - 1],
            send_sem=halo_send.at[kind, lane], recv_sem=halo_recv.at[kind, held + ahead - 1],
            device_id=whole_id(jnp.minimum(place + ahead, total - 1)), device_id_type=MESH,
        )

    goes_one = place + 1 < total
    goes_two = even & (place + 2 < total)
    plan = (
        (0, 1, goes_one),
        (0, 2, goes_two),
        (1, 1, even & (place >= 1)),
        (1, 2, goes_two & (place >= 1)),
        (2, 1, even & (place >= 2)),
    )

    def halo_start(kind, lane):
        held, ahead, active = plan[lane]

        @pl.when(active)
        def _():
            halo_copy(kind, held, ahead, lane).start()

    def halo_wait(kind, held):
        own_ref, halo = halos[kind]

        @pl.when(place >= held)
        def _():
            pltpu.make_async_remote_copy(
                src_ref=own_ref, dst_ref=halo.at[held - 1],
                send_sem=halo_send.at[kind, 0], recv_sem=halo_recv.at[kind, held - 1],
                device_id=whole_id(jnp.maximum(place - 1, 0)), device_id_type=MESH,
            ).wait_recv()

    edge = (spot == 0) | (spot == spots - 1)
    idle = place < BACK - 1
    def slab(unit, share, own):
        if unit < 2 * SLABS:
            depth = width // outers
            step = depth // SLABS
            at = pl.ds(pl.multiple_of(share * depth + (unit % SLABS) * step, step), step)
            if unit < SLABS:
                return gate_ref.at[0, at] if own else far_gate.at[at]
            return up_ref.at[0, at] if own else far_up.at[at]
        depth = hidden // outers
        at = pl.ds(pl.multiple_of(share * depth, depth), depth)
        strip = pl.ds((unit - 2 * SLABS) * wide_strip, wide_strip)
        return down_ref.at[0, at, strip] if own else far_down.at[at, strip]

    def cross_copy(unit):
        return remote(
            slab(unit, outer, True), slab(unit, outer, False), cross_send.at[unit], cross_recv.at[unit], partner
        )

    def spread_copy(unit, share, to, lane):
        part = slab(unit, share, False)
        return remote(part, part, spread_send.at[unit, lane], spread_recv.at[unit, share], inner, to)

    peers = [lax.rem(outer + step, outers) for step in range(1, outers)]

    def spread(unit):
        cross_copy(unit).wait_recv()
        for lane, to in enumerate(peers):
            spread_copy(unit, outer, to, lane).start()

    def spread_unless_idle(unit):
        if unit:
            spread(unit)
        else:
            pl.when(jnp.logical_not(idle))(lambda: spread(unit))

    def spread_wait(unit):
        for source in peers:
            spread_copy(unit, source, source, 0).wait_recv()

    def spread_sent(unit):
        for lane, to in enumerate(peers):
            spread_copy(unit, outer, to, lane).wait_send()

    def share_copy(member, slot):
        return remote(
            shares_ref.at[member], share_in.at[slot], share_send.at[member], share_recv.at[slot], 2 * base + member
        )

    def cross_point(point):
        for pace, mine in ((EDGE_PACE, edge & jnp.logical_not(idle) if point < 2 else edge), (INNER_PACE, jnp.logical_not(edge))):
            first = pace[point - 1] if point else 0
            last = pace[point] if point < len(pace) else units
            if last > first:

                @pl.when(mine)
                def _():
                    for unit in range(first, last):
                        cross_copy(unit).start()

        if point == 2:

            @pl.when(idle)
            def _():
                for unit in range(EDGE_PACE[1]):
                    cross_copy(unit).start()

    for lane in (1, 0):
        halo_start(0, lane)
    for lane in (1, 0):
        halo_start(1, lane)

    @pl.loop(1, crew)
    def _(step):
        share_copy(lax.rem(place_in_crew + step, crew), place_in_crew).start()

    share_in[place_in_crew] = shares_ref[place_in_crew]

    def one_head(held, head, wide, narrow):
        asked = query_ref[:, wide]
        asked = jnp.concatenate([asked[:, group * DH : (group + 1) * DH] for group in range(groups)], 0)
        if held == 0:
            keys, vals = key_ref[:, narrow], value_ref[:, narrow]
        else:
            keys, vals = key_halo[held - 1, :, narrow], value_halo[held - 1, :, narrow]
        scores = lax.dot_general(
            asked, keys, (((1,), (1,)), ((), ())), preferred_element_type=jnp.float32,
        ) * (math.log2(math.e) / math.sqrt(DH))
        if held == 0:
            row_id = lax.rem(lax.broadcasted_iota(jnp.int32, scores.shape, 0), tok_rows)
            col_id = lax.broadcasted_iota(jnp.int32, scores.shape, 1)
            scores = jnp.where(col_id <= row_id, scores, -jnp.inf)
        highest = jnp.max(scores, -1, keepdims=True)
        if held:
            before = top[head]
            highest = jnp.maximum(before, highest)
        expd = jnp.exp2(scores - highest).astype(jnp.bfloat16)
        counted = jnp.concatenate([vals, jnp.ones_like(vals)], 1)
        part = jnp.dot(expd, counted, preferred_element_type=jnp.float32)
        if held:
            part = part + mixed[head] * jnp.exp2(before - highest)
        top[head] = highest
        mixed[head] = part

    def attend(held):
        @pl.loop(0, KVH)
        def _(head):
            wide = pl.ds(pl.multiple_of(head * groups * DH, groups * DH), groups * DH)
            narrow = pl.ds(pl.multiple_of(head * DH, DH), DH)
            one_head(held, head, wide, narrow)

    attend(0)
    for kind in range(2):
        halo_wait(kind, 1)
        halo_start(kind, 3)
        halo_start(kind, 2)
        halo_wait(kind, 2)
        halo_start(kind, 4)

    cross_point(0)

    @pl.loop(1, crew)
    def _(step):
        source = lax.rem(place_in_crew + step, crew)
        share_copy(source, source).wait_recv()

    @pl.loop(0, crew)
    def _(member):
        row_id = lax.broadcasted_iota(jnp.int32, (tok_rows, tok_rows), 0)
        col_id = lax.broadcasted_iota(jnp.int32, (tok_rows, tok_rows), 1)
        for which in range(2):
            share = jnp.broadcast_to(share_in[member, which], (tok_rows, tok_rows))
            columns[member, which] = jnp.sum(jnp.where(row_id == col_id, share, 0.0), axis=1, keepdims=True)

    for held in range(1, BACK + 1):
        if held == 2:
            cross_point(1)
        if held == BACK:
            @pl.when(idle)
            def _():
                spread(0)

            cross_point(2)
            for unit in range(FORWARDS[0]):
                spread_unless_idle(unit)
            halo_wait(0, held)
            halo_wait(1, held)

        @pl.when(place >= held)
        def _():
            attend(held)

    cross_point(3)
    for unit in range(FORWARDS[0], FORWARDS[1]):
        spread_unless_idle(unit)

    for slot in range(QH):
        at = pl.ds(slot * DH, DH)
        own = mixed[slot // groups, slot % groups * tok_rows : (slot % groups + 1) * tok_rows]
        attended = (own[:, :DH] / own[:, DH:]).astype(jnp.bfloat16).astype(jnp.float32)
        stream[:, at] = residual_ref[:, at].astype(jnp.float32) + attended

    def row_copy(chip, k, to):
        part = rows.at[chip, core, at_piece(k)]
        return remote(part, part, row_send.at[to, k], row_recv.at[chip, k], 2 * (base + to) + core)

    def mate_copy(chip, k):
        part = rows.at[chip, core, at_piece(k)]
        return remote(part, part, mate_send.at[chip, k], mate_recv.at[chip, k], mate)

    others = [lax.rem(here + step, near) for step in range(1, near)]

    for k in range(PIECES):
        at = pl.ds(k * piece, piece)
        kept = stream[at, :]
        mean_sq = jnp.mean(kept * kept, -1, keepdims=True)
        rows[here, core, at] = (kept * lax.rsqrt(mean_sq + 1e-06) * gain_ref[...]).astype(jnp.bfloat16)
        for chip in others:
            row_copy(here, k, chip).start()
        mate_copy(here, k).start()

    cross_point(4)

    half_rows = tok_rows // HALVES

    def hide(chip, half, which):
        at = pl.ds(pl.multiple_of(half * half_rows, half_rows), half_rows)
        block = jnp.concatenate([rows[chip, side, at] for side in range(2)], 0)
        gates, ups = (far_gate, far_up) if which else (gate_ref.at[0], up_ref.at[0])
        gate_part = jnp.dot(block, gates[...], preferred_element_type=jnp.float32)
        up_part = jnp.dot(block, ups[...], preferred_element_type=jnp.float32)
        act = (gate_part / (1.0 + jnp.exp(-gate_part)) * up_part).astype(jnp.bfloat16)
        for side in range(2):
            acts[which, chip, side, at] = act[side * half_rows : (side + 1) * half_rows]

    def take_row(k):
        for chip in others:
            row_copy(chip, k, here).wait_recv()
            mate_copy(chip, k).start()

    for unit in range(FORWARDS[1], 4):
        spread_unless_idle(unit)
    for k in range(PIECES):
        mate_copy(here, k).wait_recv()
    hide(here, 0, 0)
    spread(4)
    hide(here, 1, 0)
    for unit in range(5, 2 * SLABS):
        spread(unit)
    for k in range(PIECES):
        take_row(k)
    spread(2 * SLABS)
    spread(2 * SLABS + 1)
    for chip in others:
        for k in range(PIECES):
            mate_copy(chip, k).wait_recv()
        for half in range(HALVES):
            hide(chip, half, 0)
    for unit in range(2 * SLABS):
        spread_wait(unit)
    for chip in others:
        for half in range(HALVES):
            hide(chip, half, 1)
    spread(2 * SLABS + 2)
    for half in range(HALVES):
        hide(here, half, 1)
    spread(2 * SLABS + 3)

    def give_copy(chip, strip):
        at = at_strip(strip)
        return remote(
            give.at[chip, :, at], mate_in.at[chip, :, at],
            give_send.at[chip, strip], give_recv.at[chip, strip], mate,
        )

    def back_copy(chip, slot, strip):
        at = at_strip(strip)
        return remote(
            back.at[chip, :, at], back_in.at[slot, :, at],
            back_send.at[chip, strip], back_recv.at[slot, strip], 2 * (base + chip) + core,
        )

    def part_of(chip, side, strip):
        at = at_strip(strip)
        out = None
        for which in range(2):
            downs = far_down[:, at] if which else down_ref[0, :, at]
            mine = jnp.dot(acts[which, chip, side], downs, preferred_element_type=jnp.float32)
            mine = mine.astype(jnp.bfloat16).astype(jnp.float32) * columns[2 * chip + side, which]
            out = mine if out is None else out + mine
        return out

    for strip in range(STRIPS):
        spread_wait(2 * SLABS + strip)
        at = at_strip(strip)
        for chip in others + [here]:
            give[chip, :, at] = part_of(chip, 1 - core, strip).astype(jnp.bfloat16)
            give_copy(chip, strip).start()
        for chip in others:
            mine = part_of(chip, core, strip)
            give_copy(chip, strip).wait_recv()
            back[chip, :, at] = (mine + mate_in[chip, :, at].astype(jnp.float32)).astype(jnp.bfloat16)
            back_copy(chip, here, strip).start()
        mine = part_of(here, core, strip)
        give_copy(here, strip).wait_recv()
        stream[:, at] = stream[:, at] + (mine + mate_in[here, :, at].astype(jnp.float32))

    @pl.loop(1, crew)
    def _(step):
        share_copy(lax.rem(place_in_crew + step, crew), place_in_crew).wait_send()

    for kind in range(2):
        for lane, (held, ahead, active) in enumerate(plan):

            @pl.when(active)
            def _():
                halo_copy(kind, held, ahead, lane).wait_send()

    for unit in range(units):
        cross_copy(unit).wait_send()
        spread_sent(unit)

    for k in range(PIECES):
        for chip in others:
            row_copy(here, k, chip).wait_send()
            mate_copy(chip, k).wait_send()
        mate_copy(here, k).wait_send()

    for strip in range(STRIPS):
        at = at_strip(strip)
        done = stream[:, at]
        for chip in others:
            back_copy(here, chip, strip).wait_recv()
            done = done + back_in[chip, :, at].astype(jnp.float32)
        out_ref[:, at] = done.astype(jnp.bfloat16)

    for strip in range(STRIPS):
        for chip in others:
            back_copy(chip, here, strip).wait_send()
        for chip in others + [here]:
            give_copy(chip, strip).wait_send()


def local(lanes, outers, queries, keys, values, residual, norm_gain, w_gate, w_up, w_down, routes, gates):
    tok_rows, width = queries.shape
    hidden = w_gate.shape[2]
    near = lanes // 4
    crew = 2 * near
    units = 2 * SLABS + STRIPS
    vmem = pl.BlockSpec(memory_space=pltpu.VMEM)
    dma = pltpu.SemaphoreType.DMA
    block = (tok_rows, width)
    return pl.pallas_call(
        functools.partial(layer_kernel, lanes, outers),
        out_shape=pltpu.VMEM(block, jnp.bfloat16),
        in_specs=[vmem] * 10,
        out_specs=vmem,
        scratch_shapes=[
            pltpu.VMEM((BACK,) + keys.shape, jnp.bfloat16),
            pltpu.VMEM((BACK,) + values.shape, jnp.bfloat16),
            pltpu.VMEM((KVH, QH // KVH * tok_rows, 1), jnp.float32),
            pltpu.VMEM((KVH, QH // KVH * tok_rows, 2 * DH), jnp.float32),
            pltpu.VMEM(block, jnp.float32),
            pltpu.VMEM((crew, 2, 1, tok_rows), jnp.float32),
            pltpu.VMEM((crew, 2, 1, tok_rows), jnp.float32),
            pltpu.VMEM((crew, 2, tok_rows, 1), jnp.float32),
            pltpu.VMEM((width, hidden), jnp.bfloat16),
            pltpu.VMEM((width, hidden), jnp.bfloat16),
            pltpu.VMEM((hidden, width), jnp.bfloat16),
            pltpu.VMEM((near, 2) + block, jnp.bfloat16),
            pltpu.VMEM((2, near, 2, tok_rows, hidden), jnp.bfloat16),
            pltpu.VMEM((near,) + block, jnp.bfloat16),
            pltpu.VMEM((near,) + block, jnp.bfloat16),
            pltpu.VMEM((near,) + block, jnp.bfloat16),
            pltpu.VMEM((near,) + block, jnp.bfloat16),
            dma((2, 5)), dma((2, BACK)),
            dma((crew,)), dma((crew,)),
            dma((units,)), dma((units,)),
            dma((units, outers)), dma((units, outers)),
            dma((near, PIECES)), dma((near, PIECES)),
            dma((near, PIECES)), dma((near, PIECES)),
            dma((near, STRIPS)), dma((near, STRIPS)),
            dma((near, STRIPS)), dma((near, STRIPS)),
        ],
        compiler_params=pltpu.CompilerParams(
            collective_id=0, has_side_effects=True, vmem_limit_bytes=60 * 1024 * 1024
        ),
    )(queries, keys, values, residual, norm_gain[None, :], routes.T, gates.T, w_gate, w_up, w_down)


def solution(mesh):
    return jax.shard_map(
        functools.partial(local, mesh.shape["inner"], mesh.shape["outer"]),
        mesh=mesh,
        in_specs=(
            P(("outer", "inner"), None),
            P(("outer", "inner"), None),
            P(("outer", "inner"), None),
            P(("outer", "inner"), None),
            P(),
            P("inner", None, None),
            P("inner", None, None),
            P("inner", None, None),
            P(("outer", "inner"), None),
            P(("outer", "inner"), None),
        ),
        out_specs=P(("outer", "inner"), None),
        check_vma=False,
    )
```

```python
import functools
import math

import jax
import jax.numpy as jnp
from jax import lax
from jax.experimental import pallas as pl
from jax.experimental.pallas import tpu as pltpu
from jax.sharding import PartitionSpec as P

D = 1024
QH = 8
KVH = 4
DH = 128
BACK = 3


MESH = pl.DeviceIdType.MESH
PIECES = 4
HALVES = 2
EDGE_PACE = (0,0,7,7)
INNER_PACE = (8, 8, 8, 8)
FORWARDS = (0, 0)
SLABS = 4
STRIPS = 4


def layer_kernel(
    lanes, outers, query_src, key_src, value_src, residual_src, gain_ref, route_ref, pick_ref,
    gate_src, up_src, down_src, out_ref,
    query_ref, key_ref, value_ref, residual_ref, gate_ref, up_ref, down_ref, load_sem, key_halo, value_halo, top, mixed, stream, shares_ref, share_in, columns, far_gate, far_up, far_down,
    rows, acts, give, mate_in, back, back_in,
    halo_send, halo_recv, share_send, share_recv, cross_send, cross_recv, spread_send, spread_recv,
    row_send, row_recv, mate_send, mate_recv, give_send, give_recv, back_send, back_recv,
):
    outer, inner = lax.axis_index("outer"), lax.axis_index("inner")
    total = outers * lanes
    spots = lanes // 2
    near = spots // 2
    crew = 2 * near
    spot, core = inner // 2, inner % 2
    mate = 2 * spot + (1 - core)
    base = (spot // near) * near
    here = spot - base
    place_in_crew = inner - 2 * base
    partner = lax.rem(inner + lanes // 2, lanes)
    tok_rows, width = query_src.shape
    hidden = gate_src.shape[2]
    groups = QH // KVH
    place = outer * lanes + inner
    piece = tok_rows // PIECES
    wide_strip = width // STRIPS
    units = 2 * SLABS + STRIPS

    def at_piece(k):
        return pl.ds(pl.multiple_of(k * piece, piece), piece)

    def at_strip(k):
        return pl.ds(pl.multiple_of(k * wide_strip, wide_strip), wide_strip)

    def remote(src, dst, send, recv, to, at_outer=None):
        return pltpu.make_async_remote_copy(
            src_ref=src, dst_ref=dst, send_sem=send, recv_sem=recv,
            device_id={"outer": outer if at_outer is None else at_outer, "inner": to}, device_id_type=MESH,
        )

    def whole_id(to):
        return {"outer": to // lanes, "inner": lax.rem(to, lanes)}

    loads = [
        pltpu.make_async_copy(src, dst, load_sem.at[number])
        for number, (src, dst) in enumerate((
            (query_src, query_ref), (key_src, key_ref), (value_src, value_ref), (residual_src, residual_ref),
            (gate_src, gate_ref), (up_src, up_ref), (down_src, down_ref),
        ))
    ]

    for load in loads[:3]:
        load.start()

    barrier = pltpu.get_barrier_semaphore()

    @pl.loop(1, crew)
    def _(step):
        to = 2 * base + lax.rem(place_in_crew + step, crew)
        pl.semaphore_signal(barrier, inc=1, device_id={"outer": outer, "inner": to}, device_id_type=MESH)

    pl.semaphore_signal(barrier, inc=1, device_id={"outer": outer, "inner": partner}, device_id_type=MESH)

    @pl.loop(1, outers)
    def _(step):
        to = lax.rem(outer + step, outers)
        pl.semaphore_signal(barrier, inc=1, device_id={"outer": to, "inner": inner}, device_id_type=MESH)

    expected = crew - 1 + 1 + outers - 1
    for shift in (-2, -1, 1, 2):
        other = place + shift
        reaches = (other >= 0) & (other < total)

        @pl.when(reaches)
        def _():
            pl.semaphore_signal(barrier, inc=1, device_id=whole_id(other), device_id_type=MESH)

        expected = expected + reaches.astype(jnp.int32)

    @pl.loop(0, crew)
    def _(member):
        for which in range(2):
            expert = lax.rem(2 * base + member + which * (lanes // 2), lanes)
            chosen = jnp.where(route_ref[...] == expert, pick_ref[...], 0.0)
            shares_ref[member, which] = jnp.sum(chosen, axis=0, keepdims=True)

    pl.semaphore_wait(barrier, expected)

    even = core == 0
    halos = ((key_src, key_halo), (value_src, value_halo))

    def halo_copy(kind, held, ahead, lane):
        own_ref, halo = halos[kind]
        src = own_ref if held == 0 else halo.at[held - 1]
        return pltpu.make_async_remote_copy(
            src_ref=src, dst_ref=halo.at[held + ahead - 1],
            send_sem=halo_send.at[kind, lane], recv_sem=halo_recv.at[kind, held + ahead - 1],
            device_id=whole_id(jnp.minimum(place + ahead, total - 1)), device_id_type=MESH,
        )

    goes_one = place + 1 < total
    goes_two = even & (place + 2 < total)
    plan = (
        (0, 1, goes_one),
        (0, 2, goes_two),
        (1, 1, even & (place >= 1)),
        (1, 2, goes_two & (place >= 1)),
        (2, 1, even & (place >= 2)),
    )

    def halo_start(kind, lane):
        held, ahead, active = plan[lane]

        @pl.when(active)
        def _():
            halo_copy(kind, held, ahead, lane).start()

    def halo_wait(kind, held):
        own_ref, halo = halos[kind]

        @pl.when(place >= held)
        def _():
            pltpu.make_async_remote_copy(
                src_ref=own_ref, dst_ref=halo.at[held - 1],
                send_sem=halo_send.at[kind, 0], recv_sem=halo_recv.at[kind, held - 1],
                device_id=whole_id(jnp.maximum(place - 1, 0)), device_id_type=MESH,
            ).wait_recv()

    edge = (spot == 0) | (spot == spots - 1)
    idle = place < BACK - 1
    def slab(unit, share, own):
        if unit < 2 * SLABS:
            depth = width // outers
            step = depth // SLABS
            at = pl.ds(pl.multiple_of(share * depth + (unit % SLABS) * step, step), step)
            if unit < SLABS:
                return gate_src.at[0, at] if own else far_gate.at[at]
            return up_src.at[0, at] if own else far_up.at[at]
        depth = hidden // outers
        at = pl.ds(pl.multiple_of(share * depth, depth), depth)
        strip = pl.ds((unit - 2 * SLABS) * wide_strip, wide_strip)
        return down_src.at[0, at, strip] if own else far_down.at[at, strip]

    def cross_copy(unit):
        return remote(
            slab(unit, outer, True), slab(unit, outer, False), cross_send.at[unit], cross_recv.at[unit], partner
        )

    def spread_copy(unit, share, to, lane):
        part = slab(unit, share, False)
        return remote(part, part, spread_send.at[unit, lane], spread_recv.at[unit, share], inner, to)

    peers = [lax.rem(outer + step, outers) for step in range(1, outers)]

    def spread(unit):
        cross_copy(unit).wait_recv()
        for lane, to in enumerate(peers):
            spread_copy(unit, outer, to, lane).start()

    def spread_unless_idle(unit):
        if unit:
            spread(unit)
        else:
            pl.when(jnp.logical_not(idle))(lambda: spread(unit))

    def spread_wait(unit):
        for source in peers:
            spread_copy(unit, source, source, 0).wait_recv()

    def spread_sent(unit):
        for lane, to in enumerate(peers):
            spread_copy(unit, outer, to, lane).wait_send()

    def share_copy(member, slot):
        return remote(
            shares_ref.at[member], share_in.at[slot], share_send.at[member], share_recv.at[slot], 2 * base + member
        )

    def cross_point(point):
        for pace, mine in ((EDGE_PACE, edge & jnp.logical_not(idle) if point < 2 else edge), (INNER_PACE, jnp.logical_not(edge))):
            first = pace[point - 1] if point else 0
            last = pace[point] if point < len(pace) else units
            if last > first:

                @pl.when(mine)
                def _():
                    for unit in range(first, last):
                        cross_copy(unit).start()

        if point == 2:

            @pl.when(idle)
            def _():
                for unit in range(EDGE_PACE[1]):
                    cross_copy(unit).start()

    for lane in (1, 0):
        halo_start(0, lane)
    for lane in (1, 0):
        halo_start(1, lane)

    @pl.loop(1, crew)
    def _(step):
        share_copy(lax.rem(place_in_crew + step, crew), place_in_crew).start()

    share_in[place_in_crew] = shares_ref[place_in_crew]

    def one_head(held, head, wide, narrow):
        asked = query_ref[:, wide]
        asked = jnp.concatenate([asked[:, group * DH : (group + 1) * DH] for group in range(groups)], 0)
        if held == 0:
            keys, vals = key_ref[:, narrow], value_ref[:, narrow]
        else:
            keys, vals = key_halo[held - 1, :, narrow], value_halo[held - 1, :, narrow]
        scores = lax.dot_general(
            asked, keys, (((1,), (1,)), ((), ())), preferred_element_type=jnp.float32,
        ) * (math.log2(math.e) / math.sqrt(DH))
        if held == 0:
            row_id = lax.rem(lax.broadcasted_iota(jnp.int32, scores.shape, 0), tok_rows)
            col_id = lax.broadcasted_iota(jnp.int32, scores.shape, 1)
            scores = jnp.where(col_id <= row_id, scores, -jnp.inf)
        highest = jnp.max(scores, -1, keepdims=True)
        if held:
            before = top[head]
            highest = jnp.maximum(before, highest)
        expd = jnp.exp2(scores - highest).astype(jnp.bfloat16)
        counted = jnp.concatenate([vals, jnp.ones_like(vals)], 1)
        part = jnp.dot(expd, counted, preferred_element_type=jnp.float32)
        if held:
            part = part + mixed[head] * jnp.exp2(before - highest)
        top[head] = highest
        mixed[head] = part

    def attend(held):
        @pl.loop(0, KVH)
        def _(head):
            wide = pl.ds(pl.multiple_of(head * groups * DH, groups * DH), groups * DH)
            narrow = pl.ds(pl.multiple_of(head * DH, DH), DH)
            one_head(held, head, wide, narrow)

    for load in loads[3:]:
        load.start()
    for load in loads[:4]:
        load.wait()
    attend(0)
    for kind in range(2):
        halo_wait(kind, 1)
        halo_start(kind, 3)
        halo_start(kind, 2)
        halo_wait(kind, 2)
        halo_start(kind, 4)

    cross_point(0)

    @pl.loop(1, crew)
    def _(step):
        source = lax.rem(place_in_crew + step, crew)
        share_copy(source, source).wait_recv()

    @pl.loop(0, crew)
    def _(member):
        row_id = lax.broadcasted_iota(jnp.int32, (tok_rows, tok_rows), 0)
        col_id = lax.broadcasted_iota(jnp.int32, (tok_rows, tok_rows), 1)
        for which in range(2):
            share = jnp.broadcast_to(share_in[member, which], (tok_rows, tok_rows))
            columns[member, which] = jnp.sum(jnp.where(row_id == col_id, share, 0.0), axis=1, keepdims=True)

    for held in range(1, BACK + 1):
        if held == 2:
            cross_point(1)
        if held == BACK:
            @pl.when(idle)
            def _():
                spread(0)

            cross_point(2)
            for unit in range(FORWARDS[0]):
                spread_unless_idle(unit)
            halo_wait(0, held)
            halo_wait(1, held)

        @pl.when(place >= held)
        def _():
            attend(held)

    cross_point(3)
    for unit in range(FORWARDS[0], FORWARDS[1]):
        spread_unless_idle(unit)

    for slot in range(QH):
        at = pl.ds(slot * DH, DH)
        own = mixed[slot // groups, slot % groups * tok_rows : (slot % groups + 1) * tok_rows]
        attended = (own[:, :DH] / own[:, DH:]).astype(jnp.bfloat16).astype(jnp.float32)
        stream[:, at] = residual_ref[:, at].astype(jnp.float32) + attended

    def row_copy(chip, k, to):
        part = rows.at[chip, core, at_piece(k)]
        return remote(part, part, row_send.at[to, k], row_recv.at[chip, k], 2 * (base + to) + core)

    def mate_copy(chip, k):
        part = rows.at[chip, core, at_piece(k)]
        return remote(part, part, mate_send.at[chip, k], mate_recv.at[chip, k], mate)

    others = [lax.rem(here + step, near) for step in range(1, near)]

    for k in range(PIECES):
        at = pl.ds(k * piece, piece)
        kept = stream[at, :]
        mean_sq = jnp.mean(kept * kept, -1, keepdims=True)
        rows[here, core, at] = (kept * lax.rsqrt(mean_sq + 1e-06) * gain_ref[...]).astype(jnp.bfloat16)
        for chip in others:
            row_copy(here, k, chip).start()
        mate_copy(here, k).start()

    cross_point(4)

    half_rows = tok_rows // HALVES

    def hide(chip, half, which):
        at = pl.ds(pl.multiple_of(half * half_rows, half_rows), half_rows)
        block = jnp.concatenate([rows[chip, side, at] for side in range(2)], 0)
        gates, ups = (far_gate, far_up) if which else (gate_ref.at[0], up_ref.at[0])
        gate_part = jnp.dot(block, gates[...], preferred_element_type=jnp.float32)
        up_part = jnp.dot(block, ups[...], preferred_element_type=jnp.float32)
        act = (gate_part / (1.0 + jnp.exp(-gate_part)) * up_part).astype(jnp.bfloat16)
        for side in range(2):
            acts[which, chip, side, at] = act[side * half_rows : (side + 1) * half_rows]

    def take_row(k):
        for chip in others:
            row_copy(chip, k, here).wait_recv()
            mate_copy(chip, k).start()

    for unit in range(FORWARDS[1], 4):
        spread_unless_idle(unit)
    for k in range(PIECES):
        mate_copy(here, k).wait_recv()
    for load in loads[4:]:
        load.wait()
    hide(here, 0, 0)
    spread(4)
    hide(here, 1, 0)
    for unit in range(5, 2 * SLABS):
        spread(unit)
    for k in range(PIECES):
        take_row(k)
    spread(2 * SLABS)
    spread(2 * SLABS + 1)
    for chip in others:
        for k in range(PIECES):
            mate_copy(chip, k).wait_recv()
        for half in range(HALVES):
            hide(chip, half, 0)
    for unit in range(2 * SLABS):
        spread_wait(unit)
    for chip in others:
        for half in range(HALVES):
            hide(chip, half, 1)
    spread(2 * SLABS + 2)
    spread(2 * SLABS + 3)

    def give_copy(chip, strip):
        at = at_strip(strip)
        return remote(
            give.at[chip, :, at], mate_in.at[chip, :, at],
            give_send.at[chip, strip], give_recv.at[chip, strip], mate,
        )

    def back_copy(chip, slot, strip):
        at = at_strip(strip)
        return remote(
            back.at[chip, :, at], back_in.at[slot, :, at],
            back_send.at[chip, strip], back_recv.at[slot, strip], 2 * (base + chip) + core,
        )

    def part_of(chip, side, strip):
        at = at_strip(strip)
        out = None
        for which in range(2):
            downs = far_down[:, at] if which else down_ref[0, :, at]
            mine = jnp.dot(acts[which, chip, side], downs, preferred_element_type=jnp.float32)
            mine = mine.astype(jnp.bfloat16).astype(jnp.float32) * columns[2 * chip + side, which]
            out = mine if out is None else out + mine
        return out

    def give_part(chip, strip):
        give[chip, :, at_strip(strip)] = part_of(chip, 1 - core, strip).astype(jnp.bfloat16)
        give_copy(chip, strip).start()

    def send_back(strip):
        at = at_strip(strip)
        spread_wait(2 * SLABS + strip)
        for chip in others:
            give_part(chip, strip)
        for chip in others:
            mine = part_of(chip, core, strip)
            give_copy(chip, strip).wait_recv()
            back[chip, :, at] = (mine + mate_in[chip, :, at].astype(jnp.float32)).astype(jnp.bfloat16)
            back_copy(chip, here, strip).start()

    def keep(strip):
        at = at_strip(strip)
        give_part(here, strip)
        mine = part_of(here, core, strip)
        give_copy(here, strip).wait_recv()
        stream[:, at] = stream[:, at] + (mine + mate_in[here, :, at].astype(jnp.float32))

    send_back(0)
    for half in range(HALVES):
        hide(here, half, 1)
    for strip in range(1, STRIPS):
        send_back(strip)
        keep(strip - 1)
    keep(STRIPS - 1)

    @pl.loop(1, crew)
    def _(step):
        share_copy(lax.rem(place_in_crew + step, crew), place_in_crew).wait_send()

    for kind in range(2):
        for lane, (held, ahead, active) in enumerate(plan):

            @pl.when(active)
            def _():
                halo_copy(kind, held, ahead, lane).wait_send()

    for unit in range(units):
        cross_copy(unit).wait_send()
        spread_sent(unit)

    for k in range(PIECES):
        for chip in others:
            row_copy(here, k, chip).wait_send()
            mate_copy(chip, k).wait_send()
        mate_copy(here, k).wait_send()

    for strip in range(STRIPS):
        at = at_strip(strip)
        done = stream[:, at]
        for chip in others:
            back_copy(here, chip, strip).wait_recv()
            done = done + back_in[chip, :, at].astype(jnp.float32)
        out_ref[:, at] = done.astype(jnp.bfloat16)

    for strip in range(STRIPS):
        for chip in others:
            back_copy(chip, here, strip).wait_send()
        for chip in others + [here]:
            give_copy(chip, strip).wait_send()


def local(lanes, outers, queries, keys, values, residual, norm_gain, w_gate, w_up, w_down, routes, gates):
    tok_rows, width = queries.shape
    hidden = w_gate.shape[2]
    near = lanes // 4
    crew = 2 * near
    units = 2 * SLABS + STRIPS
    vmem = pl.BlockSpec(memory_space=pltpu.VMEM)
    anywhere = pl.BlockSpec(memory_space=pl.ANY)
    dma = pltpu.SemaphoreType.DMA
    block = (tok_rows, width)
    return pl.pallas_call(
        functools.partial(layer_kernel, lanes, outers),
        out_shape=pltpu.VMEM(block, jnp.bfloat16),
        in_specs=[anywhere] * 4 + [vmem] * 3 + [anywhere] * 3,
        out_specs=vmem,
        scratch_shapes=[
            pltpu.VMEM(queries.shape, jnp.bfloat16),
            pltpu.VMEM(keys.shape, jnp.bfloat16),
            pltpu.VMEM(values.shape, jnp.bfloat16),
            pltpu.VMEM(residual.shape, jnp.bfloat16),
            pltpu.VMEM(w_gate.shape, jnp.bfloat16),
            pltpu.VMEM(w_up.shape, jnp.bfloat16),
            pltpu.VMEM(w_down.shape, jnp.bfloat16),
            dma((7,)),
            pltpu.VMEM((BACK,) + keys.shape, jnp.bfloat16),
            pltpu.VMEM((BACK,) + values.shape, jnp.bfloat16),
            pltpu.VMEM((KVH, QH // KVH * tok_rows, 1), jnp.float32),
            pltpu.VMEM((KVH, QH // KVH * tok_rows, 2 * DH), jnp.float32),
            pltpu.VMEM(block, jnp.float32),
            pltpu.VMEM((crew, 2, 1, tok_rows), jnp.float32),
            pltpu.VMEM((crew, 2, 1, tok_rows), jnp.float32),
            pltpu.VMEM((crew, 2, tok_rows, 1), jnp.float32),
            pltpu.VMEM((width, hidden), jnp.bfloat16),
            pltpu.VMEM((width, hidden), jnp.bfloat16),
            pltpu.VMEM((hidden, width), jnp.bfloat16),
            pltpu.VMEM((near, 2) + block, jnp.bfloat16),
            pltpu.VMEM((2, near, 2, tok_rows, hidden), jnp.bfloat16),
            pltpu.VMEM((near,) + block, jnp.bfloat16),
            pltpu.VMEM((near,) + block, jnp.bfloat16),
            pltpu.VMEM((near,) + block, jnp.bfloat16),
            pltpu.VMEM((near,) + block, jnp.bfloat16),
            dma((2, 5)), dma((2, BACK)),
            dma((crew,)), dma((crew,)),
            dma((units,)), dma((units,)),
            dma((units, outers)), dma((units, outers)),
            dma((near, PIECES)), dma((near, PIECES)),
            dma((near, PIECES)), dma((near, PIECES)),
            dma((near, STRIPS)), dma((near, STRIPS)),
            dma((near, STRIPS)), dma((near, STRIPS)),
        ],
        compiler_params=pltpu.CompilerParams(
            collective_id=0, has_side_effects=True, vmem_limit_bytes=60 * 1024 * 1024
        ),
    )(queries, keys, values, residual, norm_gain[None, :], routes.T, gates.T, w_gate, w_up, w_down)


def solution(mesh):
    return jax.shard_map(
        functools.partial(local, mesh.shape["inner"], mesh.shape["outer"]),
        mesh=mesh,
        in_specs=(
            P(("outer", "inner"), None),
            P(("outer", "inner"), None),
            P(("outer", "inner"), None),
            P(("outer", "inner"), None),
            P(),
            P("inner", None, None),
            P("inner", None, None),
            P("inner", None, None),
            P(("outer", "inner"), None),
            P(("outer", "inner"), None),
        ),
        out_specs=P(("outer", "inner"), None),
        check_vma=False,
    )
```

```python
import functools
import math

import jax
import jax.numpy as jnp
from jax import lax
from jax.experimental import pallas as pl
from jax.experimental.pallas import tpu as pltpu
from jax.sharding import PartitionSpec as P

D = 1024
QH = 8
KVH = 4
DH = 128
BACK = 3


MESH = pl.DeviceIdType.MESH
PIECES = 4
HALVES = 2
EDGE_PACE = (0,0,7,7)
INNER_PACE = (8, 8, 8, 8)
FORWARDS = (0, 0)
SLABS = 4
STRIPS = 4


def layer_kernel(
    lanes, outers, query_src, key_src, value_src, residual_src, gain_ref, route_ref, pick_ref,
    gate_src, up_src, down_src, out_ref,
    query_ref, key_ref, value_ref, residual_ref, gate_ref, up_ref, down_ref, load_sem, key_halo, value_halo, top, mixed, stream, shares_ref, share_in, columns, far_gate, far_up, far_down,
    rows, acts, give, mate_in, back, back_in,
    halo_send, halo_recv, share_send, share_recv, cross_send, cross_recv, spread_send, spread_recv,
    row_send, row_recv, mate_send, mate_recv, give_send, give_recv, back_send, back_recv,
):
    outer, inner = lax.axis_index("outer"), lax.axis_index("inner")
    total = outers * lanes
    spots = lanes // 2
    near = spots // 2
    crew = 2 * near
    spot, core = inner // 2, inner % 2
    mate = 2 * spot + (1 - core)
    base = (spot // near) * near
    here = spot - base
    place_in_crew = inner - 2 * base
    partner = lax.rem(inner + lanes // 2, lanes)
    tok_rows, width = query_src.shape
    hidden = gate_src.shape[2]
    groups = QH // KVH
    place = outer * lanes + inner
    piece = tok_rows // PIECES
    wide_strip = width // STRIPS
    units = 2 * SLABS + STRIPS

    def at_piece(k):
        return pl.ds(pl.multiple_of(k * piece, piece), piece)

    def at_strip(k):
        return pl.ds(pl.multiple_of(k * wide_strip, wide_strip), wide_strip)

    def remote(src, dst, send, recv, to, at_outer=None):
        return pltpu.make_async_remote_copy(
            src_ref=src, dst_ref=dst, send_sem=send, recv_sem=recv,
            device_id={"outer": outer if at_outer is None else at_outer, "inner": to}, device_id_type=MESH,
        )

    def whole_id(to):
        return {"outer": to // lanes, "inner": lax.rem(to, lanes)}

    loads = [
        pltpu.make_async_copy(src, dst, load_sem.at[number])
        for number, (src, dst) in enumerate((
            (query_src, query_ref), (key_src, key_ref), (value_src, value_ref), (residual_src, residual_ref),
            (gate_src, gate_ref), (up_src, up_ref), (down_src, down_ref),
        ))
    ]

    for load in loads[:3]:
        load.start()

    barrier = pltpu.get_barrier_semaphore()

    @pl.loop(1, crew)
    def _(step):
        to = 2 * base + lax.rem(place_in_crew + step, crew)
        pl.semaphore_signal(barrier, inc=1, device_id={"outer": outer, "inner": to}, device_id_type=MESH)

    pl.semaphore_signal(barrier, inc=1, device_id={"outer": outer, "inner": partner}, device_id_type=MESH)

    @pl.loop(1, outers)
    def _(step):
        to = lax.rem(outer + step, outers)
        pl.semaphore_signal(barrier, inc=1, device_id={"outer": to, "inner": inner}, device_id_type=MESH)

    expected = crew - 1 + 1 + outers - 1
    for shift in (-2, -1, 1, 2):
        other = place + shift
        reaches = (other >= 0) & (other < total)

        @pl.when(reaches)
        def _():
            pl.semaphore_signal(barrier, inc=1, device_id=whole_id(other), device_id_type=MESH)

        expected = expected + reaches.astype(jnp.int32)

    @pl.loop(0, crew)
    def _(member):
        for which in range(2):
            expert = lax.rem(2 * base + member + which * (lanes // 2), lanes)
            chosen = jnp.where(route_ref[...] == expert, pick_ref[...], 0.0)
            shares_ref[member, which] = jnp.sum(chosen, axis=0, keepdims=True)

    pl.semaphore_wait(barrier, expected)

    even = core == 0
    halos = ((key_src, key_halo), (value_src, value_halo))

    def halo_copy(kind, held, ahead, lane):
        own_ref, halo = halos[kind]
        src = own_ref if held == 0 else halo.at[held - 1]
        return pltpu.make_async_remote_copy(
            src_ref=src, dst_ref=halo.at[held + ahead - 1],
            send_sem=halo_send.at[kind, lane], recv_sem=halo_recv.at[kind, held + ahead - 1],
            device_id=whole_id(jnp.minimum(place + ahead, total - 1)), device_id_type=MESH,
        )

    goes_one = place + 1 < total
    goes_two = even & (place + 2 < total)
    plan = (
        (0, 1, goes_one),
        (0, 2, goes_two),
        (1, 1, even & (place >= 1)),
        (1, 2, goes_two & (place >= 1)),
        (2, 1, even & (place >= 2)),
    )

    def halo_start(kind, lane):
        held, ahead, active = plan[lane]

        @pl.when(active)
        def _():
            halo_copy(kind, held, ahead, lane).start()

    def halo_wait(kind, held):
        own_ref, halo = halos[kind]

        @pl.when(place >= held)
        def _():
            pltpu.make_async_remote_copy(
                src_ref=own_ref, dst_ref=halo.at[held - 1],
                send_sem=halo_send.at[kind, 0], recv_sem=halo_recv.at[kind, held - 1],
                device_id=whole_id(jnp.maximum(place - 1, 0)), device_id_type=MESH,
            ).wait_recv()

    edge = (spot == 0) | (spot == spots - 1)
    idle = place < BACK - 1
    def slab(unit, share, own):
        if unit < 2 * SLABS:
            depth = width // outers
            step = depth // SLABS
            at = pl.ds(pl.multiple_of(share * depth + (unit % SLABS) * step, step), step)
            if unit < SLABS:
                return gate_src.at[0, at] if own else far_gate.at[at]
            return up_src.at[0, at] if own else far_up.at[at]
        depth = hidden // outers
        at = pl.ds(pl.multiple_of(share * depth, depth), depth)
        strip = pl.ds((unit - 2 * SLABS) * wide_strip, wide_strip)
        return down_src.at[0, at, strip] if own else far_down.at[at, strip]

    def cross_copy(unit):
        return remote(
            slab(unit, outer, True), slab(unit, outer, False), cross_send.at[unit], cross_recv.at[unit], partner
        )

    def spread_copy(unit, share, to, lane):
        part = slab(unit, share, False)
        return remote(part, part, spread_send.at[unit, lane], spread_recv.at[unit, share], inner, to)

    peers = [lax.rem(outer + step, outers) for step in range(1, outers)]

    def spread(unit):
        cross_copy(unit).wait_recv()
        for lane, to in enumerate(peers):
            spread_copy(unit, outer, to, lane).start()

    def spread_unless_idle(unit):
        if unit:
            spread(unit)
        else:
            pl.when(jnp.logical_not(idle))(lambda: spread(unit))

    def spread_wait(unit):
        for source in peers:
            spread_copy(unit, source, source, 0).wait_recv()

    def spread_sent(unit):
        for lane, to in enumerate(peers):
            spread_copy(unit, outer, to, lane).wait_send()

    def share_copy(member, slot):
        return remote(
            shares_ref.at[member], share_in.at[slot], share_send.at[member], share_recv.at[slot], 2 * base + member
        )

    def cross_point(point):
        for pace, mine in ((EDGE_PACE, edge & jnp.logical_not(idle) if point < 2 else edge), (INNER_PACE, jnp.logical_not(edge))):
            first = pace[point - 1] if point else 0
            last = pace[point] if point < len(pace) else units
            if last > first:

                @pl.when(mine)
                def _():
                    for unit in range(first, last):
                        cross_copy(unit).start()

        if point == 2:

            @pl.when(idle)
            def _():
                for unit in range(EDGE_PACE[1]):
                    cross_copy(unit).start()

    for lane in (1, 0):
        halo_start(0, lane)
    for lane in (1, 0):
        halo_start(1, lane)

    @pl.loop(1, crew)
    def _(step):
        share_copy(lax.rem(place_in_crew + step, crew), place_in_crew).start()

    share_in[place_in_crew] = shares_ref[place_in_crew]

    def one_head(held, head, wide, narrow):
        asked = query_ref[:, wide]
        asked = jnp.concatenate([asked[:, group * DH : (group + 1) * DH] for group in range(groups)], 0)
        if held == 0:
            keys, vals = key_ref[:, narrow], value_ref[:, narrow]
        else:
            keys, vals = key_halo[held - 1, :, narrow], value_halo[held - 1, :, narrow]
        scores = lax.dot_general(
            asked, keys, (((1,), (1,)), ((), ())), preferred_element_type=jnp.float32,
        ) * (math.log2(math.e) / math.sqrt(DH))
        if held == 0:
            row_id = lax.rem(lax.broadcasted_iota(jnp.int32, scores.shape, 0), tok_rows)
            col_id = lax.broadcasted_iota(jnp.int32, scores.shape, 1)
            scores = jnp.where(col_id <= row_id, scores, -jnp.inf)
        highest = jnp.max(scores, -1, keepdims=True)
        if held:
            before = top[head]
            highest = jnp.maximum(before, highest)
        expd = jnp.exp2(scores - highest).astype(jnp.bfloat16)
        counted = jnp.concatenate([vals, jnp.ones_like(vals)], 1)
        part = jnp.dot(expd, counted, preferred_element_type=jnp.float32)
        if held:
            part = part + mixed[head] * jnp.exp2(before - highest)
        top[head] = highest
        mixed[head] = part

    def attend(held):
        @pl.loop(0, KVH)
        def _(head):
            wide = pl.ds(pl.multiple_of(head * groups * DH, groups * DH), groups * DH)
            narrow = pl.ds(pl.multiple_of(head * DH, DH), DH)
            one_head(held, head, wide, narrow)

    for load in loads[3:]:
        load.start()
    for load in loads[:4]:
        load.wait()
    attend(0)
    for kind in range(2):
        halo_wait(kind, 1)
        halo_start(kind, 3)
        halo_start(kind, 2)
        halo_wait(kind, 2)
        halo_start(kind, 4)

    cross_point(0)

    @pl.loop(1, crew)
    def _(step):
        source = lax.rem(place_in_crew + step, crew)
        share_copy(source, source).wait_recv()

    @pl.loop(0, crew)
    def _(member):
        row_id = lax.broadcasted_iota(jnp.int32, (tok_rows, tok_rows), 0)
        col_id = lax.broadcasted_iota(jnp.int32, (tok_rows, tok_rows), 1)
        for which in range(2):
            share = jnp.broadcast_to(share_in[member, which], (tok_rows, tok_rows))
            columns[member, which] = jnp.sum(jnp.where(row_id == col_id, share, 0.0), axis=1, keepdims=True)

    for held in range(1, BACK + 1):
        if held == 2:
            cross_point(1)
        if held == BACK:
            @pl.when(idle)
            def _():
                spread(0)

            cross_point(2)
            for unit in range(FORWARDS[0]):
                spread_unless_idle(unit)
            halo_wait(0, held)
            halo_wait(1, held)

        @pl.when(place >= held)
        def _():
            attend(held)

    cross_point(3)
    for unit in range(FORWARDS[0], FORWARDS[1]):
        spread_unless_idle(unit)

    for slot in range(QH):
        at = pl.ds(slot * DH, DH)
        own = mixed[slot // groups, slot % groups * tok_rows : (slot % groups + 1) * tok_rows]
        attended = (own[:, :DH] / own[:, DH:]).astype(jnp.bfloat16).astype(jnp.float32)
        stream[:, at] = residual_ref[:, at].astype(jnp.float32) + attended

    def row_copy(chip, k, to):
        part = rows.at[chip, core, at_piece(k)]
        return remote(part, part, row_send.at[to, k], row_recv.at[chip, k], 2 * (base + to) + core)

    def mate_copy(chip, k):
        part = rows.at[chip, core, at_piece(k)]
        return remote(part, part, mate_send.at[chip, k], mate_recv.at[chip, k], mate)

    others = [lax.rem(here + step, near) for step in range(1, near)]

    for k in range(PIECES):
        at = pl.ds(k * piece, piece)
        kept = stream[at, :]
        mean_sq = jnp.mean(kept * kept, -1, keepdims=True)
        rows[here, core, at] = (kept * lax.rsqrt(mean_sq + 1e-06) * gain_ref[...]).astype(jnp.bfloat16)
        for chip in others:
            row_copy(here, k, chip).start()
        mate_copy(here, k).start()

    cross_point(4)

    half_rows = tok_rows // HALVES

    def hide(chip, half, which):
        at = pl.ds(pl.multiple_of(half * half_rows, half_rows), half_rows)
        block = jnp.concatenate([rows[chip, side, at] for side in range(2)], 0)
        gates, ups = (far_gate, far_up) if which else (gate_ref.at[0], up_ref.at[0])
        gate_part = jnp.dot(block, gates[...], preferred_element_type=jnp.float32)
        up_part = jnp.dot(block, ups[...], preferred_element_type=jnp.float32)
        act = (gate_part / (1.0 + jnp.exp(-gate_part)) * up_part).astype(jnp.bfloat16)
        for side in range(2):
            acts[which, chip, side, at] = act[side * half_rows : (side + 1) * half_rows]

    def take_row(k):
        for chip in others:
            row_copy(chip, k, here).wait_recv()
            mate_copy(chip, k).start()

    for unit in range(FORWARDS[1], 4):
        spread_unless_idle(unit)
    for k in range(PIECES):
        mate_copy(here, k).wait_recv()
    for load in loads[4:]:
        load.wait()
    hide(here, 0, 0)
    spread(4)
    hide(here, 1, 0)
    for unit in range(5, 2 * SLABS):
        spread(unit)
    take_row(0)
    take_row(1)
    spread(2 * SLABS)
    take_row(2)
    take_row(3)
    spread(2 * SLABS + 1)
    for chip in others:
        for k in range(PIECES):
            mate_copy(chip, k).wait_recv()
        for half in range(HALVES):
            hide(chip, half, 0)
    for unit in range(2 * SLABS):
        spread_wait(unit)
    for chip in others:
        for half in range(HALVES):
            hide(chip, half, 1)
    spread(2 * SLABS + 2)
    spread(2 * SLABS + 3)

    def give_copy(chip, strip):
        at = at_strip(strip)
        return remote(
            give.at[chip, :, at], mate_in.at[chip, :, at],
            give_send.at[chip, strip], give_recv.at[chip, strip], mate,
        )

    def back_copy(chip, slot, strip):
        at = at_strip(strip)
        return remote(
            back.at[chip, :, at], back_in.at[slot, :, at],
            back_send.at[chip, strip], back_recv.at[slot, strip], 2 * (base + chip) + core,
        )

    def part_of(chip, side, strip):
        at = at_strip(strip)
        out = None
        for which in range(2):
            downs = far_down[:, at] if which else down_ref[0, :, at]
            mine = jnp.dot(acts[which, chip, side], downs, preferred_element_type=jnp.float32)
            mine = mine.astype(jnp.bfloat16).astype(jnp.float32) * columns[2 * chip + side, which]
            out = mine if out is None else out + mine
        return out

    def give_part(chip, strip):
        give[chip, :, at_strip(strip)] = part_of(chip, 1 - core, strip).astype(jnp.bfloat16)
        give_copy(chip, strip).start()

    def send_back(strip):
        at = at_strip(strip)
        spread_wait(2 * SLABS + strip)
        for chip in others:
            give_part(chip, strip)
        for chip in others:
            mine = part_of(chip, core, strip)
            give_copy(chip, strip).wait_recv()
            back[chip, :, at] = (mine + mate_in[chip, :, at].astype(jnp.float32)).astype(jnp.bfloat16)
            back_copy(chip, here, strip).start()

    def keep(strip):
        at = at_strip(strip)
        give_part(here, strip)
        mine = part_of(here, core, strip)
        give_copy(here, strip).wait_recv()
        stream[:, at] = stream[:, at] + (mine + mate_in[here, :, at].astype(jnp.float32))

    send_back(0)
    for half in range(HALVES):
        hide(here, half, 1)
    for strip in range(1, STRIPS):
        send_back(strip)
        keep(strip - 1)
    keep(STRIPS - 1)

    @pl.loop(1, crew)
    def _(step):
        share_copy(lax.rem(place_in_crew + step, crew), place_in_crew).wait_send()

    for kind in range(2):
        for lane, (held, ahead, active) in enumerate(plan):

            @pl.when(active)
            def _():
                halo_copy(kind, held, ahead, lane).wait_send()

    for unit in range(units):
        cross_copy(unit).wait_send()
        spread_sent(unit)

    for k in range(PIECES):
        for chip in others:
            row_copy(here, k, chip).wait_send()
            mate_copy(chip, k).wait_send()
        mate_copy(here, k).wait_send()

    for strip in range(STRIPS):
        at = at_strip(strip)
        done = stream[:, at]
        for chip in others:
            back_copy(here, chip, strip).wait_recv()
            done = done + back_in[chip, :, at].astype(jnp.float32)
        out_ref[:, at] = done.astype(jnp.bfloat16)

    for strip in range(STRIPS):
        for chip in others:
            back_copy(chip, here, strip).wait_send()
        for chip in others + [here]:
            give_copy(chip, strip).wait_send()


def local(lanes, outers, queries, keys, values, residual, norm_gain, w_gate, w_up, w_down, routes, gates):
    tok_rows, width = queries.shape
    hidden = w_gate.shape[2]
    near = lanes // 4
    crew = 2 * near
    units = 2 * SLABS + STRIPS
    vmem = pl.BlockSpec(memory_space=pltpu.VMEM)
    anywhere = pl.BlockSpec(memory_space=pl.ANY)
    dma = pltpu.SemaphoreType.DMA
    block = (tok_rows, width)
    return pl.pallas_call(
        functools.partial(layer_kernel, lanes, outers),
        out_shape=pltpu.VMEM(block, jnp.bfloat16),
        in_specs=[anywhere] * 4 + [vmem] * 3 + [anywhere] * 3,
        out_specs=vmem,
        scratch_shapes=[
            pltpu.VMEM(queries.shape, jnp.bfloat16),
            pltpu.VMEM(keys.shape, jnp.bfloat16),
            pltpu.VMEM(values.shape, jnp.bfloat16),
            pltpu.VMEM(residual.shape, jnp.bfloat16),
            pltpu.VMEM(w_gate.shape, jnp.bfloat16),
            pltpu.VMEM(w_up.shape, jnp.bfloat16),
            pltpu.VMEM(w_down.shape, jnp.bfloat16),
            dma((7,)),
            pltpu.VMEM((BACK,) + keys.shape, jnp.bfloat16),
            pltpu.VMEM((BACK,) + values.shape, jnp.bfloat16),
            pltpu.VMEM((KVH, QH // KVH * tok_rows, 1), jnp.float32),
            pltpu.VMEM((KVH, QH // KVH * tok_rows, 2 * DH), jnp.float32),
            pltpu.VMEM(block, jnp.float32),
            pltpu.VMEM((crew, 2, 1, tok_rows), jnp.float32),
            pltpu.VMEM((crew, 2, 1, tok_rows), jnp.float32),
            pltpu.VMEM((crew, 2, tok_rows, 1), jnp.float32),
            pltpu.VMEM((width, hidden), jnp.bfloat16),
            pltpu.VMEM((width, hidden), jnp.bfloat16),
            pltpu.VMEM((hidden, width), jnp.bfloat16),
            pltpu.VMEM((near, 2) + block, jnp.bfloat16),
            pltpu.VMEM((2, near, 2, tok_rows, hidden), jnp.bfloat16),
            pltpu.VMEM((near,) + block, jnp.bfloat16),
            pltpu.VMEM((near,) + block, jnp.bfloat16),
            pltpu.VMEM((near,) + block, jnp.bfloat16),
            pltpu.VMEM((near,) + block, jnp.bfloat16),
            dma((2, 5)), dma((2, BACK)),
            dma((crew,)), dma((crew,)),
            dma((units,)), dma((units,)),
            dma((units, outers)), dma((units, outers)),
            dma((near, PIECES)), dma((near, PIECES)),
            dma((near, PIECES)), dma((near, PIECES)),
            dma((near, STRIPS)), dma((near, STRIPS)),
            dma((near, STRIPS)), dma((near, STRIPS)),
        ],
        compiler_params=pltpu.CompilerParams(
            collective_id=0, has_side_effects=True, vmem_limit_bytes=60 * 1024 * 1024
        ),
    )(queries, keys, values, residual, norm_gain[None, :], routes.T, gates.T, w_gate, w_up, w_down)


def solution(mesh):
    return jax.shard_map(
        functools.partial(local, mesh.shape["inner"], mesh.shape["outer"]),
        mesh=mesh,
        in_specs=(
            P(("outer", "inner"), None),
            P(("outer", "inner"), None),
            P(("outer", "inner"), None),
            P(("outer", "inner"), None),
            P(),
            P("inner", None, None),
            P("inner", None, None),
            P("inner", None, None),
            P(("outer", "inner"), None),
            P(("outer", "inner"), None),
        ),
        out_specs=P(("outer", "inner"), None),
        check_vma=False,
    )
```
